32 devices in a mesh: group: 4 (over z), dev: 8 (over y, x, core).
Axes of the slice: x: 2, y: 2, z: 4, core: 2. Of those that a mesh axis runs over, the one named last changes fastest.
Arguments:
- positions: float32 [3, 1024, 256], P(None, ('group', 'dev')), may hold values from -3 to 3
- velocities: float32 [3, 1024, 256], P(None, ('group', 'dev')), may hold values from -3 to 3
- masses: float32 [1024, 256], P(('group', 'dev')), may hold values from 0.005 to 0.05
- counts: int32 [1024], P(('group', 'dev')), may hold values from 64 to 256, as said below
- walls: int32 [1024, 256], P(('group', 'dev')), may hold values 0 or 1
- neighbours: int32 [1024, 3], P(('group', 'dev')), may hold values from 0 to 55, as said below
- send_cells: int32 [4, 8, 8, 2], P('group', 'dev'), may hold values from -1 to 31, as said below
- owners: int32 [4, 256], P('group'), may hold values from 0 to 7, as said below
Outputs:
- new_state: float32 [6, 1024, 256], P(None, ('group', 'dev'))
- new_density: float32 [1024, 256], P(('group', 'dev'))
The draws below stay inside these ranges and needn't reach their ends.
Inputs may be any that keep to these rules, and one draw needn't show every extreme that they name: `counts`: every device holds at least one cell with 256 particles. `send_cells`: A device never sends to itself; slot 0 to every other device of its group holds a cell. `neighbours`: A cell never names its own row; on each device every rim row and every filled incoming slot is named at least once, and no empty incoming slot is named. `owners`: each device of a group owns exactly 32 cells afterwards; each device keeps 32 - 2 * 2 of its cells and hands exactly 2 cells to each of 2 other devices of its group, and none to the rest.
All inputs are finite; a program needn't handle non-finite values. No bound on the sum of `walls` on one device may be relied on, other than what follows from the above.
Results may differ from the reference program's by a relative error of at most 0.0003.
Values sent between devices are 32-bit elements; how exact they have to be, the bound alone decides.
A program may use at most 64 MiB of HBM per device.

```python
import math
import jax
import jax.numpy as jnp
from jax import lax

BLOCK_SIZE = 256
CELLS_DEV = 32
NEAR_CELLS = 3
RIM_CELLS = 4
SEND_SLOTS = 2
CAPACITY = 2
MOVE_SHIFTS = 2
CELLS_ALL = 1024
N_GROUP = 4
N_DEV = 8


def link_layout(key):
    base = jax.random.fold_in(key, 11)
    key_cells, key_keep, key_perm, key_local = jax.random.split(base, 4)
    shape = (N_GROUP, N_DEV, N_DEV, SEND_SLOTS)
    picked = jax.random.randint(key_cells, shape, 0, CELLS_DEV).astype(jnp.int32)
    coin = jax.random.randint(key_keep, shape, 0, 2).astype(jnp.int32)
    slot_axis = lax.broadcasted_iota(jnp.int32, shape, 3)
    source_axis = lax.broadcasted_iota(jnp.int32, shape, 1)
    target_axis = lax.broadcasted_iota(jnp.int32, shape, 2)
    keep = jnp.where(slot_axis == 0, 1, coin)
    keep = jnp.where(source_axis == target_axis, 0, keep)
    send_list = jnp.where(keep == 1, picked, -1).astype(jnp.int32)
    incoming = jnp.transpose(keep, (0, 2, 1, 3)).reshape(N_GROUP * N_DEV, N_DEV * SEND_SLOTS)
    halo_ids = 2 * RIM_CELLS + CELLS_DEV + jnp.arange(N_DEV * SEND_SLOTS, dtype=jnp.int32)
    halo_ids = jnp.where(incoming == 1, halo_ids[None, :], -1)
    rim_ids = jnp.concatenate([jnp.arange(RIM_CELLS, dtype=jnp.int32), RIM_CELLS + CELLS_DEV + jnp.arange(RIM_CELLS, dtype=jnp.int32)])
    total = CELLS_DEV * NEAR_CELLS
    filler = total - N_DEV * SEND_SLOTS - 2 * RIM_CELLS
    device_count = N_GROUP * N_DEV
    template = jnp.concatenate([halo_ids, jnp.broadcast_to(rim_ids[None, :], (device_count, 2 * RIM_CELLS)), jnp.full((device_count, filler), -1, jnp.int32)], 1)
    device_keys = jax.random.split(key_perm, device_count)
    orders = jax.vmap(lambda one_key: jax.random.permutation(one_key, total))(device_keys).astype(jnp.int32)
    shuffled = jnp.take_along_axis(template, orders, 1)
    owner_cell = lax.broadcasted_iota(jnp.int32, (device_count, total), 1) // NEAR_CELLS
    stride = jax.random.randint(key_local, (device_count, total), 1, CELLS_DEV).astype(jnp.int32)
    local_rows = RIM_CELLS + (owner_cell + stride) % CELLS_DEV
    refs = jnp.where(shuffled < 0, local_rows, shuffled).astype(jnp.int32)
    return (send_list, refs.reshape(CELLS_ALL, NEAR_CELLS))


def draw_send_cells(key, part):
    return link_layout(key)[0]


def draw_neighbours(key, part):
    return link_layout(key)[1]


def draw_owners(key, part):
    base = jax.random.fold_in(key, 23)
    key_shift, key_order = jax.random.split(base, 2)
    group_keys = jax.random.split(key_shift, N_GROUP)
    shifts = jax.vmap(lambda one_key: jax.random.permutation(one_key, N_DEV - 1)[:MOVE_SHIFTS])(group_keys).astype(jnp.int32) + 1
    movers = MOVE_SHIFTS * CAPACITY
    per_slot = jnp.concatenate([jnp.repeat(shifts, CAPACITY, axis=1), jnp.zeros((N_GROUP, CELLS_DEV - movers), jnp.int32)], 1)
    device_keys = jax.random.split(key_order, N_GROUP * N_DEV)
    orders = jax.vmap(lambda one_key: jax.random.permutation(one_key, CELLS_DEV))(device_keys).astype(jnp.int32)
    orders = orders.reshape(N_GROUP, N_DEV, CELLS_DEV)
    spread = jnp.take_along_axis(jnp.broadcast_to(per_slot[:, None, :], (N_GROUP, N_DEV, CELLS_DEV)), orders, 2)
    device_axis = lax.broadcasted_iota(jnp.int32, (N_GROUP, N_DEV, CELLS_DEV), 1)
    return ((device_axis + spread) % N_DEV).astype(jnp.int32).reshape(N_GROUP, N_DEV * CELLS_DEV)


def draw_counts(key, part):
    base = jax.random.fold_in(key, 37)
    key_count, key_full = jax.random.split(base, 2)
    device_count = N_GROUP * N_DEV
    filled = jax.random.randint(key_count, (device_count, CELLS_DEV), BLOCK_SIZE // 4, BLOCK_SIZE + 1).astype(jnp.int32)
    full_cell = jax.random.randint(key_full, (device_count, 1), 0, CELLS_DEV).astype(jnp.int32)
    cell_axis = lax.broadcasted_iota(jnp.int32, (device_count, CELLS_DEV), 1)
    filled = jnp.where(cell_axis == full_cell, BLOCK_SIZE, filled)
    return filled.reshape(CELLS_ALL).astype(jnp.int32)


def set_ends(drawn, stream_key, smallest, high):
    longest = drawn.shape.index(max(drawn.shape))
    spots = []
    for shift in (0, 1):
        where = [jax.random.randint(jax.random.fold_in(stream_key, axis), (), 0, length) for axis, length in enumerate(drawn.shape)]
        where[longest] = (where[longest] + shift) % drawn.shape[longest]
        spots.append(tuple(where))
    return drawn.at[spots[0]].set(smallest).at[spots[1]].set(high)


def block_levels(own_key, dims, cuts, least, largest):
    gain = 1.0
    for axis_at, shards_of in cuts:
        steps = jax.random.uniform(jax.random.fold_in(jax.random.fold_in(own_key, 6), axis_at), (shards_of,), jnp.float32, least / len(cuts), largest / len(cuts))
        gain = gain * jnp.repeat(jnp.exp(steps), dims[axis_at] // shards_of).reshape((-1,) + (1,) * (len(dims) - 1 - axis_at))
    return gain


def gaussian(stream_key, extent, deviation, most, cuts=(), kind=jnp.bfloat16):
    result = jax.random.normal(stream_key, extent, jnp.float32) * deviation
    if len(cuts) > 0:
        result = block_levels(stream_key, extent, cuts, -0.22, 0.18) * result
    return jnp.clip(result, min=-most, max=most).astype(kind)


def setup_inputs(seed: int = 0) -> dict:
    key_list = jax.random.split(jax.random.key(seed), 9)
    positions = gaussian(key_list[0], (3, CELLS_ALL, BLOCK_SIZE), 1.0, 3.0, ((1, 32),), jnp.float32)
    velocities = gaussian(key_list[1], (3, CELLS_ALL, BLOCK_SIZE), 0.5, 3.0, ((1, 32),), jnp.float32)
    masses = jnp.clip(jnp.exp(math.log(0.05) - 2.3025851 * jax.random.uniform(key_list[2], (CELLS_ALL, BLOCK_SIZE), jnp.float32) ** block_levels(key_list[2], (CELLS_ALL, BLOCK_SIZE), ((0, 32),), -0.2, 0.2)), 0.005, 0.05)
    counts = draw_counts(jax.random.fold_in(key_list[8], 71), 0)
    walls = set_ends((jax.random.randint(key_list[4], (CELLS_ALL, BLOCK_SIZE), 0, 4) < 1).astype(jnp.int32), jax.random.fold_in(key_list[4], 1), 0, 1)
    neighbours = draw_neighbours(jax.random.fold_in(key_list[8], 71), 0)
    send_cells = draw_send_cells(jax.random.fold_in(key_list[8], 71), 0)
    owners = draw_owners(jax.random.fold_in(key_list[8], 71), 0)
    return dict(positions=positions, velocities=velocities, masses=masses, counts=counts, walls=walls, neighbours=neighbours, send_cells=send_cells, owners=owners)


SUPPORT = 4.0
STIFFNESS = 2.0
REST_DENSITY = 0.8
VISCOSITY = 0.5
COHESION = 0.3
ADHESION = 0.8
GRAVITY = 1.0
TIME_STEP = 0.5


def pair_density(own_pos, lookup, columns):
    remote = lookup[:, columns, :]
    distance = jnp.zeros((own_pos.shape[1], own_pos.shape[2], columns.shape[1], lookup.shape[2]), jnp.float32)
    for component in range(3):
        offset = own_pos[component][:, :, None, None] - remote[component][:, None, :, :]
        distance = distance + offset * offset
    weight = jnp.maximum(1.0 - distance / SUPPORT, 0.0)
    return jnp.sum(remote[3][:, None, :, :] * weight * weight * weight, axis=(2, 3))


def pair_force(own_pos, own_vel, own_q, lookup, columns):
    remote = lookup[:, columns, :]
    distance = jnp.zeros((own_pos.shape[1], own_pos.shape[2], columns.shape[1], lookup.shape[2]), jnp.float32)
    offsets = []
    for component in range(3):
        offset = own_pos[component][:, :, None, None] - remote[component][:, None, :, :]
        offsets.append(offset)
        distance = distance + offset * offset
    weight = jnp.maximum(1.0 - distance / SUPPORT, 0.0)
    cube = weight * weight * weight
    pushes = remote[6][:, None] * (own_q[:, :, None, None] + remote[8][:, None]) * (6.0 / SUPPORT) * weight * weight - remote[7][:, None] * weight
    damping = VISCOSITY * remote[6][:, None] * cube
    total_damping = jnp.sum(damping, axis=(2, 3))
    rows = []
    for component in range(3):
        rows.append(jnp.sum(offsets[component] * pushes + damping * remote[3 + component][:, None], axis=(2, 3)) - own_vel[component] * total_damping)
    return jnp.stack(rows, 0)


def group_table(field, send_cells, group_index):
    last_group = field.shape[1] - 1
    below = lax.dynamic_index_in_dim(field, jnp.maximum(group_index - 1, 0), 1, keepdims=False)[:, :, CELLS_DEV - RIM_CELLS:]
    below = below * (group_index > 0).astype(jnp.float32)
    above = lax.dynamic_index_in_dim(field, jnp.minimum(group_index + 1, last_group), 1, keepdims=False)[:, :, :RIM_CELLS]
    above = above * (group_index < last_group).astype(jnp.float32)
    own_cells = lax.dynamic_index_in_dim(field, group_index, 1, keepdims=False)
    send_list = lax.dynamic_index_in_dim(send_cells, group_index, 0, keepdims=False)
    source = jnp.arange(N_DEV, dtype=jnp.int32)[:, None, None]
    picked = own_cells[:, source, jnp.maximum(send_list, 0)]
    picked = picked * (send_list >= 0).astype(jnp.float32)[None, :, :, :, None]
    peer_rows = jnp.transpose(picked, (0, 2, 1, 3, 4)).reshape(field.shape[0], N_DEV, N_DEV * SEND_SLOTS, BLOCK_SIZE)
    return jnp.concatenate([below, own_cells, above, peer_rows], axis=2)


def reference(positions, velocities, masses, counts, walls, neighbours, send_cells, owners):
    particle_slot = lax.broadcasted_iota(jnp.int32, (CELLS_ALL, BLOCK_SIZE), 1)
    active = (particle_slot < counts[:, None]).astype(jnp.float32)
    wall_mask = walls.astype(jnp.float32) * active
    fluid_mask = active - wall_mask
    mass_eff = masses * active
    bond = mass_eff * (COHESION + (ADHESION - COHESION) * wall_mask)
    near = neighbours.reshape(N_GROUP, N_DEV, CELLS_DEV, NEAR_CELLS)
    self_rows = RIM_CELLS + jnp.arange(CELLS_DEV, dtype=jnp.int32)

    def split_devices(field):
        return field.reshape(field.shape[0], N_GROUP, N_DEV, CELLS_DEV, BLOCK_SIZE)

    dens_field = split_devices(jnp.concatenate([positions, mass_eff[None]], 0))

    def density_group(group_index):
        lookup = group_table(dens_field, send_cells, group_index)

        def per_device(device_index):
            columns = jnp.concatenate([self_rows[:, None], near[group_index, device_index]], 1)
            return pair_density(dens_field[0:3, group_index, device_index], lookup[:, device_index], columns)

        return lax.map(per_device, jnp.arange(N_DEV, dtype=jnp.int32))

    density = lax.map(density_group, jnp.arange(N_GROUP, dtype=jnp.int32)).reshape(CELLS_ALL, BLOCK_SIZE)
    safe_rho = active * density + (1.0 - active)
    pressure_q = active * STIFFNESS * (density - REST_DENSITY) / (safe_rho * safe_rho)
    force_field = split_devices(jnp.concatenate([positions, velocities, mass_eff[None], bond[None], pressure_q[None]], 0))

    def force_group(group_index):
        lookup = group_table(force_field, send_cells, group_index)

        def per_device(device_index):
            columns = jnp.concatenate([self_rows[:, None], near[group_index, device_index]], 1)
            own_block = force_field[:, group_index, device_index]
            return pair_force(own_block[0:3], own_block[3:6], own_block[8], lookup[:, device_index], columns)

        return lax.map(per_device, jnp.arange(N_DEV, dtype=jnp.int32))

    acceleration = lax.map(force_group, jnp.arange(N_GROUP, dtype=jnp.int32))
    acceleration = jnp.transpose(acceleration, (2, 0, 1, 3, 4)).reshape(3, CELLS_ALL, BLOCK_SIZE)
    gravity_vec = jnp.array([0.0, 0.0, GRAVITY], jnp.float32)[:, None, None]
    acceleration = acceleration - gravity_vec
    new_vel = velocities + TIME_STEP * fluid_mask[None] * acceleration
    new_pos = positions + TIME_STEP * fluid_mask[None] * new_vel
    moved = jnp.concatenate([new_pos, new_vel, density[None]], 0) * active[None]
    moved = moved.reshape(7, N_GROUP, N_DEV * CELLS_DEV, BLOCK_SIZE)
    order = jnp.argsort(owners, axis=1, stable=True).astype(jnp.int32)
    settled = jnp.take_along_axis(moved, order[None, :, :, None], axis=2).reshape(7, CELLS_ALL, BLOCK_SIZE)
    return settled[0:6], settled[6]
```

```python
import functools

import jax
import jax.numpy as jnp
from jax import lax
from jax.experimental import pallas as pl
from jax.experimental.pallas import tpu as pltpu
from jax.sharding import PartitionSpec as P

RIM_CELLS = 4


SUPPORT = 4.0
STIFFNESS = 2.0
REST_DENSITY = 0.8
VISCOSITY = 0.5
COHESION = 0.3
ADHESION = 0.8
GRAVITY = 1.0
TIME_STEP = 0.5


def coarse(a):
    return a.astype(jnp.bfloat16).astype(jnp.float32)


def split3(a):
    high = coarse(a)
    rest = a - high
    mid = coarse(rest)
    return high, mid, coarse(rest - mid)


def source_side(pos, scale):
    square = jnp.sum(pos * pos, axis=0, keepdims=True)
    rows = jnp.concatenate(
        [
            scale * (1.0 - square / SUPPORT),
            scale / SUPPORT,
            scale * pos * (2.0 / SUPPORT),
            jnp.zeros_like(pos),
        ],
        0,
    )
    h, m, l = split3(rows)
    return jnp.concatenate([h, h, m, m, h, l], 0).T.astype(jnp.bfloat16)


def target_side(pos):
    square = jnp.sum(pos * pos, axis=0, keepdims=True)
    rows = jnp.concatenate([jnp.ones_like(square), -square, pos, jnp.zeros_like(pos)], 0)
    h, m, l = split3(rows)
    return jnp.concatenate([h, m, h, m, l, h], 0).astype(jnp.bfloat16)


def mm(a, b):
    return jnp.dot(a, b, preferred_element_type=jnp.float32)


def partner_rows(near, c):
    near_cells = 3
    return [RIM_CELLS + c] + [near[c * near_cells + k] for k in range(near_cells)]


def density_kernel(near, counts, table, rho_ref, q_ref, left):
    rows_total = table.shape[0]
    cells = rho_ref.shape[0]

    def prepare(r, _):
        row = table[r]
        mass = row[3:4]
        root = jnp.where(mass > 0.0, jnp.exp(jnp.log(jnp.maximum(mass, 1e-30)) * (1.0 / 3.0)), 0.0)
        left[r] = source_side(row[0:3], root)
        return 0

    lax.fori_loop(0, rows_total, prepare, 0)

    def cell(c, _):
        right = target_side(table[RIM_CELLS + c][0:3])
        total = jnp.zeros((8, right.shape[1]), jnp.float32)
        for r in partner_rows(near, c):
            u = jnp.maximum(mm(left[r], right), 0.0)
            total = total + jnp.sum((u * u * u).reshape(-1, 8, u.shape[1]), axis=0)
        rho = jnp.sum(total, axis=0, keepdims=True)
        slot = lax.broadcasted_iota(jnp.int32, rho.shape, 1)
        active = (slot < counts[c]).astype(jnp.float32)
        safe = active * rho + (1.0 - active)
        rho_ref[pl.ds(c, 1)] = rho
        q_ref[pl.ds(c, 1)] = active * STIFFNESS * (rho - REST_DENSITY) / (safe * safe)
        return 0

    lax.fori_loop(0, cells, cell, 0)


def force_kernel(near, counts, table, q_table, walls, rho_ref, out_ref, left, red1, red2, red3):
    rows_total = table.shape[0]
    cells = rho_ref.shape[0]

    def prepare(r, _):
        row = table[r]
        pos, mass, vel, bond = row[0:3], row[3:4], row[4:7], row[7:8]
        left[r] = source_side(pos, jnp.ones_like(mass))
        mq = mass * q_table[pl.ds(r, 1)]
        two = jnp.concatenate([mass, mass * pos, mq, mq * pos], 0)
        one = jnp.concatenate([bond, bond * pos, mass, mass * vel], 0)
        h2 = coarse(two)
        h1 = coarse(one)
        l1 = one - h1
        red2[r] = jnp.concatenate([h2, two - h2], 0).astype(jnp.bfloat16)
        red1[r] = jnp.concatenate([h1[0:4], l1[0:4], l1[0:4] * 0.0, l1[0:4] * 0.0], 0).astype(jnp.bfloat16)
        red3[r] = jnp.concatenate([h1[4:8], l1[4:8], l1[0:4] * 0.0, l1[0:4] * 0.0], 0).astype(jnp.bfloat16)
        return 0

    lax.fori_loop(0, rows_total, prepare, 0)

    def cell(c, _):
        row = table[RIM_CELLS + c]
        pos, vel = row[0:3], row[4:7]
        right = target_side(pos)
        width = right.shape[1]
        s1 = jnp.zeros((16, width), jnp.float32)
        s2 = jnp.zeros((16, width), jnp.float32)
        s3 = jnp.zeros((16, width), jnp.float32)
        for r in partner_rows(near, c):
            w = jnp.maximum(mm(left[r], right), 0.0)
            w2 = w * w
            w3 = w2 * w
            high = w2.astype(jnp.bfloat16)
            low = (w2 - high.astype(jnp.float32)).astype(jnp.bfloat16)
            s2 = s2 + mm(red2[r], high) + mm(red2[r], low)
            s1 = s1 + mm(red1[r], w.astype(jnp.bfloat16))
            s3 = s3 + mm(red3[r], w3.astype(jnp.bfloat16))
        s2 = s2[0:8] + s2[8:16]
        s1 = s1[0:4] + s1[4:8]
        s3 = s3[0:4] + s3[4:8]
        q = q_table[pl.ds(RIM_CELLS + c, 1)]
        acc = (
            (6.0 / SUPPORT) * (q * (pos * s2[0:1] - s2[1:4]) + (pos * s2[4:5] - s2[5:8]))
            - (pos * s1[0:1] - s1[1:4])
            + VISCOSITY * (s3[1:4] - vel * s3[0:1])
        )
        component = lax.broadcasted_iota(jnp.int32, acc.shape, 0)
        acc = acc - jnp.where(component == 2, GRAVITY, 0.0)
        slot = lax.broadcasted_iota(jnp.int32, q.shape, 1)
        active = (slot < counts[c]).astype(jnp.float32)
        fluid = active - walls[pl.ds(c, 1)].astype(jnp.float32) * active
        new_vel = vel + TIME_STEP * fluid * acc
        new_pos = pos + TIME_STEP * fluid * new_vel
        rho = rho_ref[pl.ds(c, 1)]
        out_ref[c] = active * jnp.concatenate([new_pos, new_vel, rho, jnp.zeros_like(rho)], 0)
        return 0

    lax.fori_loop(0, cells, cell, 0)


def vmem(count):
    return [pl.BlockSpec(memory_space=pltpu.VMEM)] * count


def smem(count):
    return [pl.BlockSpec(memory_space=pltpu.SMEM)] * count


def densities(near, counts, table, cells):
    rows, _, width = table.shape
    shape = jax.ShapeDtypeStruct((cells, width), jnp.float32)
    return pl.pallas_call(
        density_kernel,
        out_shape=(shape, shape),
        in_specs=smem(2) + vmem(1),
        out_specs=tuple(vmem(2)),
        scratch_shapes=[pltpu.VMEM((rows, width, 48), jnp.bfloat16)],
        compiler_params=pltpu.CompilerParams(vmem_limit_bytes=48 * 2**20),
    )(near, counts, table)


def forces(near, counts, table, q_table, walls, rho):
    rows, _, width = table.shape
    return pl.pallas_call(
        force_kernel,
        out_shape=jax.ShapeDtypeStruct((rho.shape[0], 8, width), jnp.float32),
        in_specs=smem(2) + vmem(4),
        out_specs=vmem(1)[0],
        scratch_shapes=[pltpu.VMEM((rows, width, 48), jnp.bfloat16)]
        + [pltpu.VMEM((rows, 16, width), jnp.bfloat16)] * 3,
        compiler_params=pltpu.CompilerParams(vmem_limit_bytes=48 * 2**20),
    )(near, counts, table, q_table, walls, rho)


def full_table(cells, chosen, present):
    count = lax.axis_size("group")
    below = lax.ppermute(cells[-RIM_CELLS:], "group", [(i, i + 1) for i in range(count - 1)])
    above = lax.ppermute(cells[:RIM_CELLS], "group", [(i + 1, i) for i in range(count - 1)])
    out = cells[chosen] * present.reshape((-1,) + (1,) * (cells.ndim - 1))
    arrived = lax.all_to_all(out, "dev", split_axis=0, concat_axis=0, tiled=True)
    return jnp.concatenate([below, cells, above, arrived], 0)


def shards(positions, velocities, masses, counts, walls, neighbours, send_cells, owners):
    cell_count = positions.shape[1]
    block_width = positions.shape[2]
    peer_count = lax.axis_size("dev")
    particle_slot = lax.broadcasted_iota(jnp.int32, (cell_count, block_width), 1)
    active = (particle_slot < counts[:, None]).astype(jnp.float32)
    wall_mask = walls.astype(jnp.float32) * active
    mass_eff = masses * active
    bond = mass_eff * (COHESION + (ADHESION - COHESION) * wall_mask)
    send_list = send_cells[0, 0].reshape(-1)
    present = (send_list >= 0).astype(jnp.float32)
    chosen = jnp.maximum(send_list, 0)
    fields = jnp.concatenate([positions, mass_eff[None], velocities, bond[None]], 0)
    fields = jnp.transpose(fields, (1, 0, 2))
    table = full_table(fields, chosen, present)
    near = neighbours.reshape(-1)
    density, pressure = densities(near, counts, table, cell_count)
    q_table = full_table(pressure, chosen, present)
    moved = forces(near, counts, table, q_table, walls, density)
    capacity = max(2, cell_count // (2 * peer_count))
    own_index = lax.axis_index("dev")
    group_owner = owners[0]
    own_owners = lax.dynamic_slice_in_dim(group_owner, own_index * cell_count, cell_count)
    one_hot = (own_owners[:, None] == jnp.arange(peer_count, dtype=jnp.int32)[None, :]).astype(
        jnp.int32
    )
    send_rank = jnp.sum((jnp.cumsum(one_hot, 0) - one_hot) * one_hot, 1)
    staying = own_owners == own_index
    slot_index = jnp.where(staying, peer_count * capacity, own_owners * capacity + send_rank)
    outbox = (
        jnp.zeros((peer_count * capacity, 8, block_width), jnp.float32)
        .at[slot_index]
        .set(moved, mode="drop")
    )
    inbox = lax.all_to_all(outbox, "dev", split_axis=0, concat_axis=0, tiled=True)
    arrivals = jnp.sum(
        (group_owner.reshape(peer_count, cell_count) == own_index).astype(jnp.int32), 1
    )
    arrival_start = jnp.cumsum(arrivals) - arrivals
    rank_in = lax.broadcasted_iota(jnp.int32, (peer_count, capacity), 1)
    source_row = lax.broadcasted_iota(jnp.int32, (peer_count, capacity), 0)
    usable = (rank_in < arrivals[:, None]) & (source_row != own_index)
    arrival_slot = jnp.where(usable, arrival_start[:, None] + rank_in, cell_count).reshape(-1)
    keep_slot = jnp.where(staying, arrival_start[own_index] + send_rank, cell_count)
    settled = jnp.zeros((cell_count, 8, block_width), jnp.float32)
    settled = settled.at[arrival_slot].set(inbox, mode="drop")
    settled = settled.at[keep_slot].set(moved, mode="drop")
    settled = jnp.transpose(settled, (1, 0, 2))
    return (settled[0:6], settled[6])


def solution(mesh):
    return jax.shard_map(
        shards,
        mesh=mesh,
        in_specs=(
            P(None, ("group", "dev"), None),
            P(None, ("group", "dev"), None),
            P(("group", "dev"), None),
            P(("group", "dev")),
            P(("group", "dev"), None),
            P(("group", "dev"), None),
            P("group", "dev", None, None),
            P("group", None),
        ),
        out_specs=(P(None, ("group", "dev"), None), P(("group", "dev"), None)),
        check_vma=False,
    )
```

```python
import jax
import jax.numpy as jnp
from jax import lax
from jax.experimental import pallas as pl
from jax.experimental.pallas import tpu as pltpu
from jax.sharding import PartitionSpec as P

RIM_CELLS = 4
MESH = pl.DeviceIdType.MESH


SUPPORT = 4.0
STIFFNESS = 2.0
REST_DENSITY = 0.8
VISCOSITY = 0.5
COHESION = 0.3
ADHESION = 0.8
GRAVITY = 1.0
TIME_STEP = 0.5


def coarse(a):
    return a.astype(jnp.bfloat16).astype(jnp.float32)


def split3(a):
    high = coarse(a)
    rest = a - high
    mid = coarse(rest)
    return high, mid, coarse(rest - mid)


def source_side(pos, scale):
    square = jnp.sum(pos * pos, axis=0, keepdims=True)
    rows = jnp.concatenate(
        [
            scale * (1.0 - square / SUPPORT),
            scale / SUPPORT,
            scale * pos * (2.0 / SUPPORT),
            jnp.zeros_like(pos),
        ],
        0,
    )
    h, m, l = split3(rows)
    return jnp.concatenate([h, h, m, m, h, l], 0).T.astype(jnp.bfloat16)


def target_side(pos):
    square = jnp.sum(pos * pos, axis=0, keepdims=True)
    rows = jnp.concatenate([jnp.ones_like(square), -square, pos, jnp.zeros_like(pos)], 0)
    h, m, l = split3(rows)
    return jnp.concatenate([h, m, h, m, l, h], 0).astype(jnp.bfloat16)


def mm(a, b):
    return jnp.dot(a, b, preferred_element_type=jnp.float32)


def partner_rows(near, c):
    near_cells = 3
    return [RIM_CELLS + c] + [near[c * near_cells + k] for k in range(near_cells)]


def to_peers(act):
    me, count = lax.axis_index("dev"), lax.axis_size("dev")

    def one(k, _):
        act(lax.rem(me + k, count))
        return 0

    lax.fori_loop(1, count, one, 0)


def greet(rim):
    barrier = pltpu.get_barrier_semaphore()
    group, groups = lax.axis_index("group"), lax.axis_size("group")

    def hello(p):
        pl.semaphore_signal(barrier, inc=1, device_id={"dev": p}, device_id_type=MESH)

    to_peers(hello)
    if not rim:
        pl.semaphore_wait(barrier, lax.axis_size("dev") - 1)
        return

    @pl.when(group > 0)
    def _():
        pl.semaphore_signal(barrier, inc=1, device_id={"group": group - 1}, device_id_type=MESH)

    @pl.when(group < groups - 1)
    def _():
        pl.semaphore_signal(barrier, inc=1, device_id={"group": group + 1}, device_id_type=MESH)

    sides = jnp.where(group > 0, 1, 0) + jnp.where(group < groups - 1, 1, 0)
    pl.semaphore_wait(barrier, lax.axis_size("dev") - 1 + sides)


def swap_slots(source, target, base, width, send_sem, recv_sem):
    me = lax.axis_index("dev")

    def copy(p, lands):
        return pltpu.make_async_remote_copy(
            src_ref=source.at[pl.ds(p * width, width)],
            dst_ref=target.at[pl.ds(base + lands * width, width)],
            send_sem=send_sem.at[p],
            recv_sem=recv_sem.at[lands],
            device_id={"dev": p},
            device_id_type=MESH,
        )

    def finish():
        to_peers(lambda p: copy(p, p).wait_recv())
        to_peers(lambda p: copy(p, me).wait_send())

    to_peers(lambda p: copy(p, me).start())
    return finish


def swap_rims(table, cells, sems):
    group, groups = lax.axis_index("group"), lax.axis_size("group")

    def copy(up):
        source = cells if up else RIM_CELLS
        lands = 0 if up else RIM_CELLS + cells
        step = 1 if up else -1
        return pltpu.make_async_remote_copy(
            src_ref=table.at[pl.ds(source, RIM_CELLS)],
            dst_ref=table.at[pl.ds(lands, RIM_CELLS)],
            send_sem=sems.at[0 if up else 1],
            recv_sem=sems.at[2 if up else 3],
            device_id={"group": group + step},
            device_id_type=MESH,
        )

    @pl.when(group < groups - 1)
    def _():
        copy(True).start()

    @pl.when(group > 0)
    def _():
        copy(False).start()

    def finish():
        @pl.when(group < groups - 1)
        def _():
            copy(False).wait_recv()
            copy(True).wait_send()

        @pl.when(group > 0)
        def _():
            copy(True).wait_recv()
            copy(False).wait_send()

    return finish


def clear_missing(table, cells):
    group, groups = lax.axis_index("group"), lax.axis_size("group")
    shape = (RIM_CELLS,) + table.shape[1:]

    @pl.when(group == 0)
    def _():
        table[0:RIM_CELLS] = jnp.zeros(shape, jnp.float32)

    @pl.when(group == groups - 1)
    def _():
        table[RIM_CELLS + cells : 2 * RIM_CELLS + cells] = jnp.zeros(shape, jnp.float32)


def clear_own(table, base, width):
    table[pl.ds(base + lax.axis_index("dev") * width, width)] = jnp.zeros(
        (width,) + table.shape[1:], jnp.float32
    )


def fields_kernel(counts, sends, pos, vel, masses, walls, table, out, slot_send, slot_recv, rim_sem):
    cells = masses.shape[0]
    slots = out.shape[0]
    base = cells + 2 * RIM_CELLS
    width = slots // lax.axis_size("dev")

    def rows(c):
        mass = masses[pl.ds(c, 1)]
        slot = lax.broadcasted_iota(jnp.int32, mass.shape, 1)
        active = (slot < counts[c]).astype(jnp.float32)
        mass = mass * active
        wall = walls[pl.ds(c, 1)].astype(jnp.float32) * active
        bond = mass * (COHESION + (ADHESION - COHESION) * wall)
        place = [pos[f, pl.ds(c, 1)] for f in range(3)]
        speed = [vel[f, pl.ds(c, 1)] for f in range(3)]
        return jnp.concatenate(place + [mass] + speed + [bond], 0)

    def own(c, _):
        table[RIM_CELLS + c] = rows(c)
        return 0

    def listed(s, _):
        c = sends[s]
        out[s] = rows(jnp.maximum(c, 0)) * (c >= 0).astype(jnp.float32)
        return 0

    lax.fori_loop(0, slots, listed, 0)
    lax.fori_loop(0, cells, own, 0)
    clear_missing(table, cells)
    clear_own(table, base, width)
    greet(True)
    done_slots = swap_slots(out, table, base, width, slot_send, slot_recv)
    done_rims = swap_rims(table, cells, rim_sem)
    done_slots()
    done_rims()


def pressure_kernel(sends, pressure, table, out, slot_send, slot_recv, rim_sem):
    cells = pressure.shape[0]
    slots = out.shape[0]
    base = cells + 2 * RIM_CELLS
    width = slots // lax.axis_size("dev")

    def listed(s, _):
        c = sends[s]
        out[s] = pressure[jnp.maximum(c, 0)] * (c >= 0).astype(jnp.float32)
        return 0

    def own(c, _):
        table[RIM_CELLS + c] = pressure[c]
        return 0

    lax.fori_loop(0, slots, listed, 0)
    lax.fori_loop(0, cells, own, 0)
    clear_missing(table, cells)
    clear_own(table, base, width)
    greet(True)
    done_slots = swap_slots(out, table, base, width, slot_send, slot_recv)
    done_rims = swap_rims(table, cells, rim_sem)
    done_slots()
    done_rims()


def settle_kernel(picks, order, moved, state, rho, out, pool, slot_send, slot_recv):
    cells = moved.shape[0]
    slots = out.shape[0]
    width = slots // lax.axis_size("dev")

    def listed(s, _):
        out[s] = moved[picks[s]]
        return 0

    def own(c, _):
        pool[c] = moved[c]
        return 0

    lax.fori_loop(0, slots, listed, 0)
    lax.fori_loop(0, cells, own, 0)
    clear_own(pool, cells, width)
    greet(False)
    swap_slots(out, pool, cells, width, slot_send, slot_recv)()

    def place(s, _):
        row = pool[order[s]]
        for f in range(6):
            state[f, pl.ds(s, 1)] = row[f : f + 1]
        rho[pl.ds(s, 1)] = row[6:7]
        return 0

    lax.fori_loop(0, cells, place, 0)


def density_kernel(near, counts, table, rho_ref, q_ref, left):
    rows_total = table.shape[0]
    cells = rho_ref.shape[0]

    def prepare(r, _):
        row = table[r]
        mass = row[3:4]
        root = jnp.where(mass > 0.0, jnp.exp(jnp.log(jnp.maximum(mass, 1e-30)) * (1.0 / 3.0)), 0.0)
        left[r] = source_side(row[0:3], root)
        return 0

    lax.fori_loop(0, rows_total, prepare, 0)

    def cell(c, _):
        right = target_side(table[RIM_CELLS + c][0:3])
        total = jnp.zeros((8, right.shape[1]), jnp.float32)
        for r in partner_rows(near, c):
            u = jnp.maximum(mm(left[r], right), 0.0)
            total = total + jnp.sum((u * u * u).reshape(-1, 8, u.shape[1]), axis=0)
        rho = jnp.sum(total, axis=0, keepdims=True)
        slot = lax.broadcasted_iota(jnp.int32, rho.shape, 1)
        active = (slot < counts[c]).astype(jnp.float32)
        safe = active * rho + (1.0 - active)
        rho_ref[c] = rho
        q_ref[c] = active * STIFFNESS * (rho - REST_DENSITY) / (safe * safe)
        return 0

    lax.fori_loop(0, cells, cell, 0)


def force_kernel(near, counts, table, q_table, walls, rho_ref, out_ref, left, red1, red2, red3):
    rows_total = table.shape[0]
    cells = rho_ref.shape[0]

    def prepare(r, _):
        row = table[r]
        pos, mass, vel, bond = row[0:3], row[3:4], row[4:7], row[7:8]
        left[r] = source_side(pos, jnp.ones_like(mass))
        mq = mass * q_table[r]
        two = jnp.concatenate([mass, mass * pos, mq, mq * pos], 0)
        one = jnp.concatenate([bond, bond * pos, mass, mass * vel], 0)
        h2 = coarse(two)
        h1 = coarse(one)
        l1 = one - h1
        red2[r] = jnp.concatenate([h2, two - h2], 0).astype(jnp.bfloat16)
        red1[r] = jnp.concatenate([h1[0:4], l1[0:4], l1[0:4] * 0.0, l1[0:4] * 0.0], 0).astype(jnp.bfloat16)
        red3[r] = jnp.concatenate([h1[4:8], l1[4:8], l1[0:4] * 0.0, l1[0:4] * 0.0], 0).astype(jnp.bfloat16)
        return 0

    lax.fori_loop(0, rows_total, prepare, 0)

    def cell(c, _):
        row = table[RIM_CELLS + c]
        pos, vel = row[0:3], row[4:7]
        right = target_side(pos)
        width = right.shape[1]
        s1 = jnp.zeros((16, width), jnp.float32)
        s2 = jnp.zeros((16, width), jnp.float32)
        s3 = jnp.zeros((16, width), jnp.float32)
        for r in partner_rows(near, c):
            w = jnp.maximum(mm(left[r], right), 0.0)
            w2 = w * w
            w3 = w2 * w
            high = w2.astype(jnp.bfloat16)
            low = (w2 - high.astype(jnp.float32)).astype(jnp.bfloat16)
            s2 = s2 + mm(red2[r], high) + mm(red2[r], low)
            s1 = s1 + mm(red1[r], w.astype(jnp.bfloat16))
            s3 = s3 + mm(red3[r], w3.astype(jnp.bfloat16))
        s2 = s2[0:8] + s2[8:16]
        s1 = s1[0:4] + s1[4:8]
        s3 = s3[0:4] + s3[4:8]
        q = q_table[RIM_CELLS + c]
        acc = (
            (6.0 / SUPPORT) * (q * (pos * s2[0:1] - s2[1:4]) + (pos * s2[4:5] - s2[5:8]))
            - (pos * s1[0:1] - s1[1:4])
            + VISCOSITY * (s3[1:4] - vel * s3[0:1])
        )
        component = lax.broadcasted_iota(jnp.int32, acc.shape, 0)
        acc = acc - jnp.where(component == 2, GRAVITY, 0.0)
        slot = lax.broadcasted_iota(jnp.int32, q.shape, 1)
        active = (slot < counts[c]).astype(jnp.float32)
        fluid = active - walls[pl.ds(c, 1)].astype(jnp.float32) * active
        new_vel = vel + TIME_STEP * fluid * acc
        new_pos = pos + TIME_STEP * fluid * new_vel
        rho = rho_ref[c]
        out_ref[c] = active * jnp.concatenate([new_pos, new_vel, rho, jnp.zeros_like(rho)], 0)
        return 0

    lax.fori_loop(0, cells, cell, 0)


def vmem(count):
    return [pl.BlockSpec(memory_space=pltpu.VMEM)] * count


def smem(count):
    return [pl.BlockSpec(memory_space=pltpu.SMEM)] * count


def densities(near, counts, table, cells):
    rows, _, width = table.shape
    shape = jax.ShapeDtypeStruct((cells, 1, width), jnp.float32)
    return pl.pallas_call(
        density_kernel,
        out_shape=(shape, shape),
        in_specs=smem(2) + vmem(1),
        out_specs=tuple(vmem(2)),
        scratch_shapes=[pltpu.VMEM((rows, width, 48), jnp.bfloat16)],
        compiler_params=pltpu.CompilerParams(vmem_limit_bytes=48 * 2**20),
    )(near, counts, table)


def forces(near, counts, table, q_table, walls, rho):
    rows, _, width = table.shape
    return pl.pallas_call(
        force_kernel,
        out_shape=jax.ShapeDtypeStruct((rho.shape[0], 8, width), jnp.float32),
        in_specs=smem(2) + vmem(4),
        out_specs=vmem(1)[0],
        scratch_shapes=[pltpu.VMEM((rows, width, 48), jnp.bfloat16)]
        + [pltpu.VMEM((rows, 16, width), jnp.bfloat16)] * 3,
        compiler_params=pltpu.CompilerParams(vmem_limit_bytes=48 * 2**20),
    )(near, counts, table, q_table, walls, rho)


def remote(kernel, collective_id, in_specs, out_shape, scratch):
    single = not isinstance(out_shape, tuple)
    return pl.pallas_call(
        kernel,
        out_shape=out_shape,
        in_specs=in_specs,
        out_specs=vmem(1)[0] if single else tuple(vmem(len(out_shape))),
        scratch_shapes=scratch,
        compiler_params=pltpu.CompilerParams(
            collective_id=collective_id, has_side_effects=True, vmem_limit_bytes=32 * 2**20
        ),
    )


def shards(positions, velocities, masses, counts, walls, neighbours, send_cells, owners):
    cells = positions.shape[1]
    width = positions.shape[2]
    peer_count = lax.axis_size("dev")
    me = lax.axis_index("dev")
    f32 = jnp.float32
    sends = send_cells.reshape(-1)
    slots = sends.shape[0]
    rows = 2 * RIM_CELLS + cells + slots
    near = neighbours.reshape(-1)
    dma = pltpu.SemaphoreType.DMA
    sems = [dma((peer_count,)), dma((peer_count,)), dma((4,))]

    capacity = max(2, cells // (2 * peer_count))
    everyone = owners[0]
    mine = lax.dynamic_slice_in_dim(everyone, me * cells, cells)
    index = jnp.arange(cells, dtype=jnp.int32)
    earlier = (mine[None, :] == mine[:, None]) & (index[None, :] < index[:, None])
    key = mine * cells + jnp.sum(earlier.astype(jnp.int32), 1)
    slot = jnp.arange(peer_count * capacity, dtype=jnp.int32)
    wanted = slot // capacity * cells + slot % capacity
    picks = jnp.sum(jnp.where(key[None, :] == wanted[:, None], index[None, :], 0), 1)
    comes = everyone.reshape(peer_count, cells) == me
    rank = jnp.sum(
        (comes[:, None, :] & (index[None, None, :] < index[None, :, None])).astype(jnp.int32), 2
    )
    amounts = jnp.sum(comes.astype(jnp.int32), 1)
    device = jnp.arange(peer_count, dtype=jnp.int32)
    starts = jnp.sum(jnp.where(device[None, :] < device[:, None], amounts[None, :], 0), 1)
    code = jnp.where(
        (device == me)[:, None], index[None, :], cells + device[:, None] * capacity + rank
    )
    goal = jnp.where(comes, starts[:, None] + rank, -1)
    order = jnp.sum(
        jnp.where(goal.reshape(1, -1) == index[:, None], code.reshape(1, -1), 0), 1
    )

    table = remote(
        fields_kernel,
        1,
        smem(2) + vmem(4),
        jax.ShapeDtypeStruct((rows, 8, width), f32),
        [pltpu.VMEM((slots, 8, width), f32)] + sems,
    )(counts, sends, positions, velocities, masses, walls)
    density, pressure = densities(near, counts, table, cells)
    q_table = remote(
        pressure_kernel,
        2,
        smem(1) + vmem(1),
        jax.ShapeDtypeStruct((rows, 1, width), f32),
        [pltpu.VMEM((slots, 1, width), f32)] + sems,
    )(sends, pressure)
    moved = forces(near, counts, table, q_table, walls, density)
    return remote(
        settle_kernel,
        3,
        smem(2) + vmem(1),
        (jax.ShapeDtypeStruct((6, cells, width), f32), jax.ShapeDtypeStruct((cells, width), f32)),
        [
            pltpu.VMEM((peer_count * capacity, 8, width), f32),
            pltpu.VMEM((cells + peer_count * capacity, 8, width), f32),
        ]
        + sems[:2],
    )(picks, order, moved)


def solution(mesh):
    return jax.shard_map(
        shards,
        mesh=mesh,
        in_specs=(
            P(None, ("group", "dev"), None),
            P(None, ("group", "dev"), None),
            P(("group", "dev"), None),
            P(("group", "dev")),
            P(("group", "dev"), None),
            P(("group", "dev"), None),
            P("group", "dev", None, None),
            P("group", None),
        ),
        out_specs=(P(None, ("group", "dev"), None), P(("group", "dev"), None)),
        check_vma=False,
    )
```

```python
import jax
import jax.numpy as jnp
from jax import lax
from jax.experimental import pallas as pl
from jax.experimental.pallas import tpu as pltpu
from jax.sharding import PartitionSpec as P

RIM_CELLS = 4
MESH = pl.DeviceIdType.MESH


SUPPORT = 4.0
STIFFNESS = 2.0
REST_DENSITY = 0.8
VISCOSITY = 0.5
COHESION = 0.3
ADHESION = 0.8
GRAVITY = 1.0
TIME_STEP = 0.5


def coarse(a):
    return a.astype(jnp.bfloat16).astype(jnp.float32)


def split3(a):
    high = coarse(a)
    rest = a - high
    mid = coarse(rest)
    return high, mid, coarse(rest - mid)


def source_side(pos, scale):
    square = jnp.sum(pos * pos, axis=0, keepdims=True)
    rows = jnp.concatenate(
        [
            scale * (1.0 - square / SUPPORT),
            scale / SUPPORT,
            scale * pos * (2.0 / SUPPORT),
            jnp.zeros_like(pos),
        ],
        0,
    )
    h, m, l = split3(rows)
    return jnp.concatenate([h, h, m, m, h, l], 0).T.astype(jnp.bfloat16)


def target_side(pos):
    square = jnp.sum(pos * pos, axis=0, keepdims=True)
    rows = jnp.concatenate([jnp.ones_like(square), -square, pos, jnp.zeros_like(pos)], 0)
    h, m, l = split3(rows)
    return jnp.concatenate([h, m, h, m, l, h], 0).astype(jnp.bfloat16)


def mm(a, b):
    return jnp.dot(a, b, preferred_element_type=jnp.float32)


HALF = 128
NEAR = 3
CLASSES = [(width, n) for width in (1, 2) for n in range(NEAR + width, 2 * NEAR + width + 1)]


def sort_cells(near, filled, lists, sizes, extra):
    cells = near.shape[0] // NEAR
    base = 2 * (NEAR + 1)
    for k in range(base * 2):
        sizes[k] = 0

    def one(c, _):
        own = filled[RIM_CELLS + c]
        count = 0
        for r in [RIM_CELLS + c] + [near[c * NEAR + k] for k in range(NEAR)]:
            extra[c * 4 + count] = r
            count = count + filled[r]
        cls = own * (NEAR + 1) + count - own
        size = sizes[cls]
        lists[cls * cells + size] = c
        sizes[cls] = size + 1
        return 0

    lax.fori_loop(0, cells, one, 0)


def by_class(lists, sizes, body, together):
    cells = lists.shape[0] // len(CLASSES)
    for cls, (width, n) in enumerate(CLASSES):
        size = sizes[cls]

        def step(k, _, cls=cls, width=width, n=n, size=size):
            for u in range(together):
                at = jnp.minimum(k * together + u, size - 1)
                body(lists[cls * cells + at], width * HALF, n)
            return 0

        lax.fori_loop(0, (size + together - 1) // together, step, 0)


def chunks(near, extra, c, n):
    rows = [RIM_CELLS + c] + [near[c * NEAR + k] for k in range(NEAR)]
    return [2 * r for r in rows] + [2 * extra[c * 4 + k] + 1 for k in range(n - NEAR - 1)]


def widen(row, width):
    if row.shape[1] == width:
        return row
    return jnp.concatenate([row, jnp.zeros((row.shape[0], width - row.shape[1]), row.dtype)], 1)


def to_peers(act):
    me, count = lax.axis_index("dev"), lax.axis_size("dev")

    def one(k, _):
        act(lax.rem(me + k, count))
        return 0

    lax.fori_loop(1, count, one, 0)


def greet(rim):
    barrier = pltpu.get_barrier_semaphore()
    group, groups = lax.axis_index("group"), lax.axis_size("group")

    def hello(p):
        pl.semaphore_signal(barrier, inc=1, device_id={"dev": p}, device_id_type=MESH)

    to_peers(hello)
    if not rim:
        pl.semaphore_wait(barrier, lax.axis_size("dev") - 1)
        return

    @pl.when(group > 0)
    def _():
        pl.semaphore_signal(barrier, inc=1, device_id={"group": group - 1}, device_id_type=MESH)

    @pl.when(group < groups - 1)
    def _():
        pl.semaphore_signal(barrier, inc=1, device_id={"group": group + 1}, device_id_type=MESH)

    sides = jnp.where(group > 0, 1, 0) + jnp.where(group < groups - 1, 1, 0)
    pl.semaphore_wait(barrier, lax.axis_size("dev") - 1 + sides)


def swap_slots(source, target, base, width, send_sem, recv_sem):
    me = lax.axis_index("dev")

    def copy(p, lands):
        return pltpu.make_async_remote_copy(
            src_ref=source.at[pl.ds(p * width, width)],
            dst_ref=target.at[pl.ds(base + lands * width, width)],
            send_sem=send_sem.at[p],
            recv_sem=recv_sem.at[lands],
            device_id={"dev": p},
            device_id_type=MESH,
        )

    def finish():
        to_peers(lambda p: copy(p, p).wait_recv())
        to_peers(lambda p: copy(p, me).wait_send())

    to_peers(lambda p: copy(p, me).start())
    return finish


def swap_rims(table, cells, sems):
    group, groups = lax.axis_index("group"), lax.axis_size("group")

    def copy(up):
        source = cells if up else RIM_CELLS
        lands = 0 if up else RIM_CELLS + cells
        step = 1 if up else -1
        return pltpu.make_async_remote_copy(
            src_ref=table.at[pl.ds(source, RIM_CELLS)],
            dst_ref=table.at[pl.ds(lands, RIM_CELLS)],
            send_sem=sems.at[0 if up else 1],
            recv_sem=sems.at[2 if up else 3],
            device_id={"group": group + step},
            device_id_type=MESH,
        )

    @pl.when(group < groups - 1)
    def _():
        copy(True).start()

    @pl.when(group > 0)
    def _():
        copy(False).start()

    def finish():
        @pl.when(group < groups - 1)
        def _():
            copy(False).wait_recv()
            copy(True).wait_send()

        @pl.when(group > 0)
        def _():
            copy(True).wait_recv()
            copy(False).wait_send()

    return finish


def clear_missing(table, cells):
    group, groups = lax.axis_index("group"), lax.axis_size("group")
    shape = (RIM_CELLS,) + table.shape[1:]

    @pl.when(group == 0)
    def _():
        table[0:RIM_CELLS] = jnp.zeros(shape, jnp.float32)

    @pl.when(group == groups - 1)
    def _():
        table[RIM_CELLS + cells : 2 * RIM_CELLS + cells] = jnp.zeros(shape, jnp.float32)


def clear_own(table, base, width):
    table[pl.ds(base + lax.axis_index("dev") * width, width)] = jnp.zeros(
        (width,) + table.shape[1:], jnp.float32
    )


def fields_kernel(counts, sends, pos, vel, masses, walls, table, out, slot_send, slot_recv, rim_sem):
    cells = masses.shape[0]
    slots = out.shape[0]
    base = cells + 2 * RIM_CELLS
    width = slots // lax.axis_size("dev")

    def rows(c):
        mass = masses[pl.ds(c, 1)]
        slot = lax.broadcasted_iota(jnp.int32, mass.shape, 1)
        active = (slot < counts[c]).astype(jnp.float32)
        mass = mass * active
        wall = walls[pl.ds(c, 1)].astype(jnp.float32) * active
        bond = mass * (COHESION + (ADHESION - COHESION) * wall)
        place = [pos[f, pl.ds(c, 1)] for f in range(3)]
        speed = [vel[f, pl.ds(c, 1)] for f in range(3)]
        return jnp.concatenate(place + [mass] + speed + [bond], 0)

    def own(c, _):
        table[RIM_CELLS + c] = rows(c)
        return 0

    def listed(s, _):
        c = sends[s]
        out[s] = rows(jnp.maximum(c, 0)) * (c >= 0).astype(jnp.float32)
        return 0

    lax.fori_loop(0, slots, listed, 0)
    lax.fori_loop(0, cells, own, 0)
    clear_missing(table, cells)
    clear_own(table, base, width)
    greet(True)
    done_slots = swap_slots(out, table, base, width, slot_send, slot_recv)
    done_rims = swap_rims(table, cells, rim_sem)
    done_slots()
    done_rims()


def pressure_kernel(sends, pressure, table, out, slot_send, slot_recv, rim_sem):
    cells = pressure.shape[0]
    slots = out.shape[0]
    base = cells + 2 * RIM_CELLS
    width = slots // lax.axis_size("dev")

    def listed(s, _):
        c = sends[s]
        out[s] = pressure[jnp.maximum(c, 0)] * (c >= 0).astype(jnp.float32)
        return 0

    def own(c, _):
        table[RIM_CELLS + c] = pressure[c]
        return 0

    lax.fori_loop(0, slots, listed, 0)
    lax.fori_loop(0, cells, own, 0)
    clear_missing(table, cells)
    clear_own(table, base, width)
    greet(True)
    done_slots = swap_slots(out, table, base, width, slot_send, slot_recv)
    done_rims = swap_rims(table, cells, rim_sem)
    done_slots()
    done_rims()


def settle_kernel(picks, order, moved, state, rho, out, pool, slot_send, slot_recv):
    cells = moved.shape[0]
    slots = out.shape[0]
    width = slots // lax.axis_size("dev")

    def listed(s, _):
        out[s] = moved[picks[s]]
        return 0

    def own(c, _):
        pool[c] = moved[c]
        return 0

    lax.fori_loop(0, slots, listed, 0)
    lax.fori_loop(0, cells, own, 0)
    clear_own(pool, cells, width)
    greet(False)
    swap_slots(out, pool, cells, width, slot_send, slot_recv)()

    def place(s, _):
        row = pool[order[s]]
        for f in range(6):
            state[f, pl.ds(s, 1)] = row[f : f + 1]
        rho[pl.ds(s, 1)] = row[6:7]
        return 0

    lax.fori_loop(0, cells, place, 0)


def density_kernel(near, counts, filled, table, rho_ref, q_ref, lists, sizes, extra, left):
    rows_total = table.shape[0]
    full = table.shape[2]
    sort_cells(near, filled, lists, sizes, extra)

    def prepare(r, _):
        row = table[r]
        mass = row[3:4]
        root = jnp.where(mass > 0.0, jnp.exp(jnp.log(jnp.maximum(mass, 1e-30)) * (1.0 / 3.0)), 0.0)
        side = source_side(row[0:3], root)
        left[2 * r] = side[:HALF]
        left[2 * r + 1] = side[HALF:]
        return 0

    lax.fori_loop(0, rows_total, prepare, 0, unroll=8)

    def cell(c, width, n):
        right = target_side(table[RIM_CELLS + c][0:3, :width])
        total = jnp.zeros((8, width), jnp.float32)
        for k in chunks(near, extra, c, n):
            u = jnp.maximum(mm(left[k], right), 0.0)
            total = total + jnp.sum((u * u * u).reshape(-1, 8, width), axis=0)
        rho = jnp.sum(total, axis=0, keepdims=True)
        slot = lax.broadcasted_iota(jnp.int32, rho.shape, 1)
        active = (slot < counts[c]).astype(jnp.float32)
        safe = active * rho + (1.0 - active)
        rho_ref[c] = widen(rho, full)
        q_ref[c] = widen(active * STIFFNESS * (rho - REST_DENSITY) / (safe * safe), full)

    by_class(lists, sizes, cell, 2)


def force_kernel(
    near, counts, lists, sizes, extra, table, q_table, walls, rho_ref, out_ref, left, red1, red2, red3
):
    rows_total = table.shape[0]
    full = table.shape[2]

    def prepare(r, _):
        row = table[r]
        pos, mass, vel, bond = row[0:3], row[3:4], row[4:7], row[7:8]
        side = source_side(pos, jnp.ones_like(mass))
        mq = mass * q_table[r]
        two = jnp.concatenate([mass, mass * pos, mq, mq * pos], 0)
        one = jnp.concatenate([bond, bond * pos, mass, mass * vel], 0)
        h2 = coarse(two)
        h1 = coarse(one)
        l1 = one - h1
        none = jnp.zeros_like(one)
        r2 = jnp.concatenate([h2, two - h2], 0).astype(jnp.bfloat16)
        r1 = jnp.concatenate([h1[0:4], l1[0:4], none], 0).astype(jnp.bfloat16)
        r3 = jnp.concatenate([h1[4:8], l1[4:8], none], 0).astype(jnp.bfloat16)
        for k in range(2):
            part = slice(k * HALF, (k + 1) * HALF)
            left[2 * r + k] = side[part]
            red1[2 * r + k] = r1[:, part]
            red2[2 * r + k] = r2[:, part]
            red3[2 * r + k] = r3[:, part]
        return 0

    lax.fori_loop(0, rows_total, prepare, 0, unroll=8)

    def cell(c, width, n):
        row = table[RIM_CELLS + c][:, :width]
        pos, vel = row[0:3], row[4:7]
        right = target_side(pos)
        s1 = jnp.zeros((16, width), jnp.float32)
        s2 = jnp.zeros((16, width), jnp.float32)
        s3 = jnp.zeros((16, width), jnp.float32)
        for k in chunks(near, extra, c, n):
            w = jnp.maximum(mm(left[k], right), 0.0)
            w2 = w * w
            w3 = w2 * w
            high = w2.astype(jnp.bfloat16)
            low = (w2 - high.astype(jnp.float32)).astype(jnp.bfloat16)
            s2 = s2 + mm(red2[k], high) + mm(red2[k], low)
            s1 = s1 + mm(red1[k], w.astype(jnp.bfloat16))
            s3 = s3 + mm(red3[k], w3.astype(jnp.bfloat16))
        s2 = s2[0:8] + s2[8:16]
        s1 = s1[0:4] + s1[4:8]
        s3 = s3[0:4] + s3[4:8]
        q = q_table[RIM_CELLS + c][:, :width]
        acc = (
            (6.0 / SUPPORT) * (q * (pos * s2[0:1] - s2[1:4]) + (pos * s2[4:5] - s2[5:8]))
            - (pos * s1[0:1] - s1[1:4])
            + VISCOSITY * (s3[1:4] - vel * s3[0:1])
        )
        component = lax.broadcasted_iota(jnp.int32, acc.shape, 0)
        acc = acc - jnp.where(component == 2, GRAVITY, 0.0)
        slot = lax.broadcasted_iota(jnp.int32, q.shape, 1)
        active = (slot < counts[c]).astype(jnp.float32)
        fluid = active - walls[pl.ds(c, 1)][:, :width].astype(jnp.float32) * active
        new_vel = vel + TIME_STEP * fluid * acc
        new_pos = pos + TIME_STEP * fluid * new_vel
        rho = rho_ref[c][:, :width]
        out_ref[c] = widen(
            active * jnp.concatenate([new_pos, new_vel, rho, jnp.zeros_like(rho)], 0), full
        )

    by_class(lists, sizes, cell, 1)


def vmem(count):
    return [pl.BlockSpec(memory_space=pltpu.VMEM)] * count


def smem(count):
    return [pl.BlockSpec(memory_space=pltpu.SMEM)] * count


def densities(near, counts, filled, table, cells):
    rows, _, width = table.shape
    shape = jax.ShapeDtypeStruct((cells, 1, width), jnp.float32)
    plan = [(len(CLASSES) * cells,), (4 * (NEAR + 1),), (4 * cells,)]
    return pl.pallas_call(
        density_kernel,
        out_shape=(shape, shape) + tuple(jax.ShapeDtypeStruct(p, jnp.int32) for p in plan),
        in_specs=smem(3) + vmem(1),
        out_specs=tuple(vmem(2) + smem(3)),
        scratch_shapes=[pltpu.VMEM((rows * 2, HALF, 48), jnp.bfloat16)],
        compiler_params=pltpu.CompilerParams(vmem_limit_bytes=48 * 2**20),
    )(near, counts, filled, table)


def forces(near, counts, plan, table, q_table, walls, rho):
    rows, _, width = table.shape
    return pl.pallas_call(
        force_kernel,
        out_shape=jax.ShapeDtypeStruct((rho.shape[0], 8, width), jnp.float32),
        in_specs=smem(5) + vmem(4),
        out_specs=vmem(1)[0],
        scratch_shapes=[pltpu.VMEM((rows * 2, HALF, 48), jnp.bfloat16)]
        + [pltpu.VMEM((rows * 2, 16, HALF), jnp.bfloat16)] * 3,
        compiler_params=pltpu.CompilerParams(vmem_limit_bytes=48 * 2**20),
    )(near, counts, *plan, table, q_table, walls, rho)


def remote(kernel, collective_id, in_specs, out_shape, scratch):
    single = not isinstance(out_shape, tuple)
    return pl.pallas_call(
        kernel,
        out_shape=out_shape,
        in_specs=in_specs,
        out_specs=vmem(1)[0] if single else tuple(vmem(len(out_shape))),
        scratch_shapes=scratch,
        compiler_params=pltpu.CompilerParams(
            collective_id=collective_id, has_side_effects=True, vmem_limit_bytes=32 * 2**20
        ),
    )


def shards(positions, velocities, masses, counts, walls, neighbours, send_cells, owners):
    cells = positions.shape[1]
    width = positions.shape[2]
    peer_count = lax.axis_size("dev")
    me = lax.axis_index("dev")
    f32 = jnp.float32
    sends = send_cells.reshape(-1)
    slots = sends.shape[0]
    rows = 2 * RIM_CELLS + cells + slots
    near = neighbours.reshape(-1)
    dma = pltpu.SemaphoreType.DMA
    sems = [dma((peer_count,)), dma((peer_count,)), dma((4,))]

    capacity = max(2, cells // (2 * peer_count))
    everyone = owners[0]
    mine = lax.dynamic_slice_in_dim(everyone, me * cells, cells)
    index = jnp.arange(cells, dtype=jnp.int32)
    earlier = (mine[None, :] == mine[:, None]) & (index[None, :] < index[:, None])
    key = mine * cells + jnp.sum(earlier.astype(jnp.int32), 1)
    slot = jnp.arange(peer_count * capacity, dtype=jnp.int32)
    wanted = slot // capacity * cells + slot % capacity
    picks = jnp.sum(jnp.where(key[None, :] == wanted[:, None], index[None, :], 0), 1)
    comes = everyone.reshape(peer_count, cells) == me
    rank = jnp.sum(
        (comes[:, None, :] & (index[None, None, :] < index[None, :, None])).astype(jnp.int32), 2
    )
    amounts = jnp.sum(comes.astype(jnp.int32), 1)
    device = jnp.arange(peer_count, dtype=jnp.int32)
    starts = jnp.sum(jnp.where(device[None, :] < device[:, None], amounts[None, :], 0), 1)
    code = jnp.where(
        (device == me)[:, None], index[None, :], cells + device[:, None] * capacity + rank
    )
    goal = jnp.where(comes, starts[:, None] + rank, -1)
    order = jnp.sum(
        jnp.where(goal.reshape(1, -1) == index[:, None], code.reshape(1, -1), 0), 1
    )

    table = remote(
        fields_kernel,
        1,
        smem(2) + vmem(4),
        jax.ShapeDtypeStruct((rows, 8, width), f32),
        [pltpu.VMEM((slots, 8, width), f32)] + sems,
    )(counts, sends, positions, velocities, masses, walls)
    filled = jnp.any(table[:, 3, HALF:] != 0.0, axis=1).astype(jnp.int32)
    density, pressure, *plan = densities(near, counts, filled, table, cells)
    q_table = remote(
        pressure_kernel,
        2,
        smem(1) + vmem(1),
        jax.ShapeDtypeStruct((rows, 1, width), f32),
        [pltpu.VMEM((slots, 1, width), f32)] + sems,
    )(sends, pressure)
    moved = forces(near, counts, plan, table, q_table, walls, density)
    return remote(
        settle_kernel,
        3,
        smem(2) + vmem(1),
        (jax.ShapeDtypeStruct((6, cells, width), f32), jax.ShapeDtypeStruct((cells, width), f32)),
        [
            pltpu.VMEM((peer_count * capacity, 8, width), f32),
            pltpu.VMEM((cells + peer_count * capacity, 8, width), f32),
        ]
        + sems[:2],
    )(picks, order, moved)


def solution(mesh):
    return jax.shard_map(
        shards,
        mesh=mesh,
        in_specs=(
            P(None, ("group", "dev"), None),
            P(None, ("group", "dev"), None),
            P(("group", "dev"), None),
            P(("group", "dev")),
            P(("group", "dev"), None),
            P(("group", "dev"), None),
            P("group", "dev", None, None),
            P("group", None),
        ),
        out_specs=(P(None, ("group", "dev"), None), P(("group", "dev"), None)),
        check_vma=False,
    )
```

```python
import jax
import jax.numpy as jnp
from jax import lax
from jax.experimental import pallas as pl
from jax.experimental.pallas import tpu as pltpu
from jax.sharding import PartitionSpec as P

RIM_CELLS = 4
MESH = pl.DeviceIdType.MESH


SUPPORT = 4.0
STIFFNESS = 2.0
REST_DENSITY = 0.8
VISCOSITY = 0.5
COHESION = 0.3
ADHESION = 0.8
GRAVITY = 1.0
TIME_STEP = 0.5


def coarse(a):
    return a.astype(jnp.bfloat16).astype(jnp.float32)


def split3(a):
    high = coarse(a)
    rest = a - high
    mid = coarse(rest)
    return high, mid, coarse(rest - mid)


def source_side(pos, scale):
    square = jnp.sum(pos * pos, axis=0, keepdims=True)
    rows = jnp.concatenate(
        [
            scale * (1.0 - square / SUPPORT),
            scale / SUPPORT,
            scale * pos * (2.0 / SUPPORT),
            jnp.zeros_like(pos),
        ],
        0,
    )
    h, m, l = split3(rows)
    return jnp.concatenate([h, h, m, m, h, l], 0).T.astype(jnp.bfloat16)


def target_side(pos):
    square = jnp.sum(pos * pos, axis=0, keepdims=True)
    rows = jnp.concatenate([jnp.ones_like(square), -square, pos, jnp.zeros_like(pos)], 0)
    h, m, l = split3(rows)
    return jnp.concatenate([h, m, h, m, l, h], 0).astype(jnp.bfloat16)


def mm(a, b):
    return jnp.dot(a, b, preferred_element_type=jnp.float32)


HALF = 128
NEAR = 3
CLASSES = [(width, n) for width in (1, 2) for n in range(NEAR + width, 2 * NEAR + width + 1)]


def sort_cells(near, filled, lists, sizes, extra):
    cells = near.shape[0] // NEAR
    base = 2 * (NEAR + 1)
    for k in range(base * 2):
        sizes[k] = 0

    def one(c, _):
        own = filled[RIM_CELLS + c]
        count = 0
        for r in [RIM_CELLS + c] + [near[c * NEAR + k] for k in range(NEAR)]:
            extra[c * 4 + count] = r
            count = count + filled[r]
        cls = own * (NEAR + 1) + count - own
        size = sizes[cls]
        lists[cls * cells + size] = c
        sizes[cls] = size + 1
        return 0

    lax.fori_loop(0, cells, one, 0)


def by_class(lists, sizes, body, together):
    cells = lists.shape[0] // len(CLASSES)
    for cls, (width, n) in enumerate(CLASSES):
        size = sizes[cls]

        def step(k, _, cls=cls, width=width, n=n, size=size):
            for u in range(together):
                at = jnp.minimum(k * together + u, size - 1)
                body(lists[cls * cells + at], width * HALF, n)
            return 0

        lax.fori_loop(0, (size + together - 1) // together, step, 0)


def chunks(near, extra, c, n):
    rows = [RIM_CELLS + c] + [near[c * NEAR + k] for k in range(NEAR)]
    return [2 * r for r in rows] + [2 * extra[c * 4 + k] + 1 for k in range(n - NEAR - 1)]


def widen(row, width):
    if row.shape[1] == width:
        return row
    return jnp.concatenate([row, jnp.zeros((row.shape[0], width - row.shape[1]), row.dtype)], 1)


def to_peers(act):
    me, count = lax.axis_index("dev"), lax.axis_size("dev")

    def one(k, _):
        act(lax.rem(me + k, count))
        return 0

    lax.fori_loop(1, count, one, 0)


def greet(rim):
    barrier = pltpu.get_barrier_semaphore()
    group, groups = lax.axis_index("group"), lax.axis_size("group")

    def hello(p):
        pl.semaphore_signal(barrier, inc=1, device_id={"dev": p}, device_id_type=MESH)

    to_peers(hello)
    if not rim:
        pl.semaphore_wait(barrier, lax.axis_size("dev") - 1)
        return

    @pl.when(group > 0)
    def _():
        pl.semaphore_signal(barrier, inc=1, device_id={"group": group - 1}, device_id_type=MESH)

    @pl.when(group < groups - 1)
    def _():
        pl.semaphore_signal(barrier, inc=1, device_id={"group": group + 1}, device_id_type=MESH)

    sides = jnp.where(group > 0, 1, 0) + jnp.where(group < groups - 1, 1, 0)
    pl.semaphore_wait(barrier, lax.axis_size("dev") - 1 + sides)


def swap_slots(source, target, base, width, send_sem, recv_sem):
    me = lax.axis_index("dev")

    def copy(p, lands):
        return pltpu.make_async_remote_copy(
            src_ref=source.at[pl.ds(p * width, width)],
            dst_ref=target.at[pl.ds(base + lands * width, width)],
            send_sem=send_sem.at[p],
            recv_sem=recv_sem.at[lands],
            device_id={"dev": p},
            device_id_type=MESH,
        )

    def finish():
        to_peers(lambda p: copy(p, p).wait_recv())
        to_peers(lambda p: copy(p, me).wait_send())

    to_peers(lambda p: copy(p, me).start())
    return finish


def swap_rims(table, cells, sems):
    group, groups = lax.axis_index("group"), lax.axis_size("group")

    def copy(up):
        source = cells if up else RIM_CELLS
        lands = 0 if up else RIM_CELLS + cells
        step = 1 if up else -1
        return pltpu.make_async_remote_copy(
            src_ref=table.at[pl.ds(source, RIM_CELLS)],
            dst_ref=table.at[pl.ds(lands, RIM_CELLS)],
            send_sem=sems.at[0 if up else 1],
            recv_sem=sems.at[2 if up else 3],
            device_id={"group": group + step},
            device_id_type=MESH,
        )

    @pl.when(group < groups - 1)
    def _():
        copy(True).start()

    @pl.when(group > 0)
    def _():
        copy(False).start()

    def finish():
        @pl.when(group < groups - 1)
        def _():
            copy(False).wait_recv()
            copy(True).wait_send()

        @pl.when(group > 0)
        def _():
            copy(True).wait_recv()
            copy(False).wait_send()

    return finish


def clear_missing(table, cells):
    group, groups = lax.axis_index("group"), lax.axis_size("group")
    shape = (RIM_CELLS,) + table.shape[1:]

    @pl.when(group == 0)
    def _():
        table[0:RIM_CELLS] = jnp.zeros(shape, jnp.float32)

    @pl.when(group == groups - 1)
    def _():
        table[RIM_CELLS + cells : 2 * RIM_CELLS + cells] = jnp.zeros(shape, jnp.float32)


def clear_own(table, base, width):
    table[pl.ds(base + lax.axis_index("dev") * width, width)] = jnp.zeros(
        (width,) + table.shape[1:], jnp.float32
    )


def fields_kernel(counts, sends, pos, vel, masses, walls, table, out, slot_send, slot_recv, rim_sem):
    cells = masses.shape[0]
    slots = out.shape[0]
    base = cells + 2 * RIM_CELLS
    width = slots // lax.axis_size("dev")

    def rows(c):
        mass = masses[pl.ds(c, 1)]
        slot = lax.broadcasted_iota(jnp.int32, mass.shape, 1)
        active = (slot < counts[c]).astype(jnp.float32)
        mass = mass * active
        wall = walls[pl.ds(c, 1)].astype(jnp.float32) * active
        bond = mass * (COHESION + (ADHESION - COHESION) * wall)
        place = [pos[f, pl.ds(c, 1)] for f in range(3)]
        speed = [vel[f, pl.ds(c, 1)] for f in range(3)]
        return jnp.concatenate(place + [mass] + speed + [bond], 0)

    def own(c, _):
        table[RIM_CELLS + c] = rows(c)
        return 0

    def listed(s, _):
        c = sends[s]
        out[s] = rows(jnp.maximum(c, 0)) * (c >= 0).astype(jnp.float32)
        return 0

    lax.fori_loop(0, slots, listed, 0)
    lax.fori_loop(0, cells, own, 0)
    clear_missing(table, cells)
    clear_own(table, base, width)
    greet(True)
    done_slots = swap_slots(out, table, base, width, slot_send, slot_recv)
    done_rims = swap_rims(table, cells, rim_sem)
    done_slots()
    done_rims()


def pressure_kernel(sends, pressure, table, out, slot_send, slot_recv, rim_sem):
    cells = pressure.shape[0]
    slots = out.shape[0]
    base = cells + 2 * RIM_CELLS
    width = slots // lax.axis_size("dev")

    def listed(s, _):
        c = sends[s]
        out[s] = pressure[jnp.maximum(c, 0)] * (c >= 0).astype(jnp.float32)
        return 0

    def own(c, _):
        table[RIM_CELLS + c] = pressure[c]
        return 0

    lax.fori_loop(0, slots, listed, 0)
    lax.fori_loop(0, cells, own, 0)
    clear_missing(table, cells)
    clear_own(table, base, width)
    greet(True)
    done_slots = swap_slots(out, table, base, width, slot_send, slot_recv)
    done_rims = swap_rims(table, cells, rim_sem)
    done_slots()
    done_rims()


def settle_kernel(picks, order, moved, state, rho, out, pool, slot_send, slot_recv):
    cells = moved.shape[0]
    slots = out.shape[0]
    width = slots // lax.axis_size("dev")

    def listed(s, _):
        out[s] = moved[picks[s]]
        return 0

    def own(c, _):
        pool[c] = moved[c]
        return 0

    lax.fori_loop(0, slots, listed, 0)
    lax.fori_loop(0, cells, own, 0)
    clear_own(pool, cells, width)
    greet(False)
    swap_slots(out, pool, cells, width, slot_send, slot_recv)()

    def place(s, _):
        row = pool[order[s]]
        for f in range(6):
            state[f, pl.ds(s, 1)] = row[f : f + 1]
        rho[pl.ds(s, 1)] = row[6:7]
        return 0

    lax.fori_loop(0, cells, place, 0)


def density_kernel(near, counts, filled, table, rho_ref, q_ref, lists, sizes, extra, left):
    rows_total = table.shape[0]
    full = table.shape[2]
    sort_cells(near, filled, lists, sizes, extra)

    def prepare(r, _):
        row = table[r]
        mass = row[3:4]
        root = jnp.where(mass > 0.0, jnp.exp(jnp.log(jnp.maximum(mass, 1e-30)) * (1.0 / 3.0)), 0.0)
        side = source_side(row[0:3], root)
        left[2 * r] = side[:HALF]
        left[2 * r + 1] = side[HALF:]
        return 0

    lax.fori_loop(0, rows_total, prepare, 0, unroll=8)

    def cell(c, width, n):
        right = target_side(table[RIM_CELLS + c][0:3, :width])
        total = jnp.zeros((8, width), jnp.float32)
        for k in chunks(near, extra, c, n):
            u = jnp.maximum(mm(left[k], right), 0.0)
            total = total + jnp.sum((u * u * u).reshape(-1, 8, width), axis=0)
        rho = jnp.sum(total, axis=0, keepdims=True)
        slot = lax.broadcasted_iota(jnp.int32, rho.shape, 1)
        active = (slot < counts[c]).astype(jnp.float32)
        safe = active * rho + (1.0 - active)
        rho_ref[c] = widen(rho, full)
        q_ref[c] = widen(active * STIFFNESS * (rho - REST_DENSITY) / (safe * safe), full)

    by_class(lists, sizes, cell, 2)


def force_kernel(
    near, counts, lists, sizes, extra, table, q_table, walls, rho_ref, out_ref, left, red_a, red_b
):
    rows_total = table.shape[0]
    full = table.shape[2]

    def prepare(r, _):
        row = table[r]
        pos, mass, vel, bond = row[0:3], row[3:4], row[4:7], row[7:8]
        side = source_side(pos, jnp.ones_like(mass))
        mq = mass * q_table[r]
        two = jnp.concatenate([mass, mass * pos, mq, mq * pos], 0)
        one = jnp.concatenate([bond, bond * pos, mass, mass * vel], 0)
        h2 = coarse(two)
        h1 = coarse(one)
        l1 = one - h1
        r2 = jnp.concatenate([h2, two - h2], 0)
        r1 = jnp.concatenate([h1[0:4], l1[0:4]], 0)
        r3 = jnp.concatenate([h1[4:8], l1[4:8]], 0)
        none = jnp.zeros((8, HALF), jnp.float32)
        for k in range(2):
            part = slice(k * HALF, (k + 1) * HALF)
            left[2 * r + k] = side[part]
            red_a[2 * r + k] = jnp.concatenate([r2[:, part]] * 2, 1).astype(jnp.bfloat16)
            red_b[2 * r + k] = jnp.concatenate(
                [jnp.concatenate([r1[:, part], none], 1), jnp.concatenate([none, r3[:, part]], 1)], 0
            ).astype(jnp.bfloat16)
        return 0

    lax.fori_loop(0, rows_total, prepare, 0, unroll=8)

    def cell(c, width, n):
        row = table[RIM_CELLS + c][:, :width]
        pos, vel = row[0:3], row[4:7]
        right = target_side(pos)
        s2 = jnp.zeros((16, width), jnp.float32)
        s13 = jnp.zeros((16, width), jnp.float32)
        for k in chunks(near, extra, c, n):
            w = jnp.maximum(mm(left[k], right), 0.0)
            w2 = w * w
            w3 = w2 * w
            high = w2.astype(jnp.bfloat16)
            low = (w2 - high.astype(jnp.float32)).astype(jnp.bfloat16)
            pair_a = jnp.concatenate([high, low], 0)
            pair_b = jnp.concatenate([w.astype(jnp.bfloat16), w3.astype(jnp.bfloat16)], 0)
            if width == HALF:
                both = mm(
                    jnp.concatenate([red_a[k], red_b[k]], 0), jnp.concatenate([pair_a, pair_b], 1)
                )
                s2 = s2 + both[:16, :HALF]
                s13 = s13 + both[16:, HALF:]
            else:
                s2 = s2 + mm(red_a[k], pair_a)
                s13 = s13 + mm(red_b[k], pair_b)
        s1, s3 = s13[0:8], s13[8:16]
        s2 = s2[0:8] + s2[8:16]
        s1 = s1[0:4] + s1[4:8]
        s3 = s3[0:4] + s3[4:8]
        q = q_table[RIM_CELLS + c][:, :width]
        acc = (
            (6.0 / SUPPORT) * (q * (pos * s2[0:1] - s2[1:4]) + (pos * s2[4:5] - s2[5:8]))
            - (pos * s1[0:1] - s1[1:4])
            + VISCOSITY * (s3[1:4] - vel * s3[0:1])
        )
        component = lax.broadcasted_iota(jnp.int32, acc.shape, 0)
        acc = acc - jnp.where(component == 2, GRAVITY, 0.0)
        slot = lax.broadcasted_iota(jnp.int32, q.shape, 1)
        active = (slot < counts[c]).astype(jnp.float32)
        fluid = active - walls[pl.ds(c, 1)][:, :width].astype(jnp.float32) * active
        new_vel = vel + TIME_STEP * fluid * acc
        new_pos = pos + TIME_STEP * fluid * new_vel
        rho = rho_ref[c][:, :width]
        out_ref[c] = widen(
            active * jnp.concatenate([new_pos, new_vel, rho, jnp.zeros_like(rho)], 0), full
        )

    by_class(lists, sizes, cell, 1)


def vmem(count):
    return [pl.BlockSpec(memory_space=pltpu.VMEM)] * count


def smem(count):
    return [pl.BlockSpec(memory_space=pltpu.SMEM)] * count


def densities(near, counts, filled, table, cells):
    rows, _, width = table.shape
    shape = jax.ShapeDtypeStruct((cells, 1, width), jnp.float32)
    plan = [(len(CLASSES) * cells,), (4 * (NEAR + 1),), (4 * cells,)]
    return pl.pallas_call(
        density_kernel,
        out_shape=(shape, shape) + tuple(jax.ShapeDtypeStruct(p, jnp.int32) for p in plan),
        in_specs=smem(3) + vmem(1),
        out_specs=tuple(vmem(2) + smem(3)),
        scratch_shapes=[pltpu.VMEM((rows * 2, HALF, 48), jnp.bfloat16)],
        compiler_params=pltpu.CompilerParams(vmem_limit_bytes=48 * 2**20),
    )(near, counts, filled, table)


def forces(near, counts, plan, table, q_table, walls, rho):
    rows, _, width = table.shape
    return pl.pallas_call(
        force_kernel,
        out_shape=jax.ShapeDtypeStruct((rho.shape[0], 8, width), jnp.float32),
        in_specs=smem(5) + vmem(4),
        out_specs=vmem(1)[0],
        scratch_shapes=[pltpu.VMEM((rows * 2, HALF, 48), jnp.bfloat16)]
        + [pltpu.VMEM((rows * 2, 16, 2 * HALF), jnp.bfloat16)] * 2,
        compiler_params=pltpu.CompilerParams(vmem_limit_bytes=48 * 2**20),
    )(near, counts, *plan, table, q_table, walls, rho)


def remote(kernel, collective_id, in_specs, out_shape, scratch):
    single = not isinstance(out_shape, tuple)
    return pl.pallas_call(
        kernel,
        out_shape=out_shape,
        in_specs=in_specs,
        out_specs=vmem(1)[0] if single else tuple(vmem(len(out_shape))),
        scratch_shapes=scratch,
        compiler_params=pltpu.CompilerParams(
            collective_id=collective_id, has_side_effects=True, vmem_limit_bytes=32 * 2**20
        ),
    )


def shards(positions, velocities, masses, counts, walls, neighbours, send_cells, owners):
    cells = positions.shape[1]
    width = positions.shape[2]
    peer_count = lax.axis_size("dev")
    me = lax.axis_index("dev")
    f32 = jnp.float32
    sends = send_cells.reshape(-1)
    slots = sends.shape[0]
    rows = 2 * RIM_CELLS + cells + slots
    near = neighbours.reshape(-1)
    dma = pltpu.SemaphoreType.DMA
    sems = [dma((peer_count,)), dma((peer_count,)), dma((4,))]

    capacity = max(2, cells // (2 * peer_count))
    everyone = owners[0]
    mine = lax.dynamic_slice_in_dim(everyone, me * cells, cells)
    index = jnp.arange(cells, dtype=jnp.int32)
    earlier = (mine[None, :] == mine[:, None]) & (index[None, :] < index[:, None])
    key = mine * cells + jnp.sum(earlier.astype(jnp.int32), 1)
    slot = jnp.arange(peer_count * capacity, dtype=jnp.int32)
    wanted = slot // capacity * cells + slot % capacity
    picks = jnp.sum(jnp.where(key[None, :] == wanted[:, None], index[None, :], 0), 1)
    comes = everyone.reshape(peer_count, cells) == me
    rank = jnp.sum(
        (comes[:, None, :] & (index[None, None, :] < index[None, :, None])).astype(jnp.int32), 2
    )
    amounts = jnp.sum(comes.astype(jnp.int32), 1)
    device = jnp.arange(peer_count, dtype=jnp.int32)
    starts = jnp.sum(jnp.where(device[None, :] < device[:, None], amounts[None, :], 0), 1)
    code = jnp.where(
        (device == me)[:, None], index[None, :], cells + device[:, None] * capacity + rank
    )
    goal = jnp.where(comes, starts[:, None] + rank, -1)
    order = jnp.sum(
        jnp.where(goal.reshape(1, -1) == index[:, None], code.reshape(1, -1), 0), 1
    )

    table = remote(
        fields_kernel,
        1,
        smem(2) + vmem(4),
        jax.ShapeDtypeStruct((rows, 8, width), f32),
        [pltpu.VMEM((slots, 8, width), f32)] + sems,
    )(counts, sends, positions, velocities, masses, walls)
    filled = jnp.any(table[:, 3, HALF:] != 0.0, axis=1).astype(jnp.int32)
    density, pressure, *plan = densities(near, counts, filled, table, cells)
    q_table = remote(
        pressure_kernel,
        2,
        smem(1) + vmem(1),
        jax.ShapeDtypeStruct((rows, 1, width), f32),
        [pltpu.VMEM((slots, 1, width), f32)] + sems,
    )(sends, pressure)
    moved = forces(near, counts, plan, table, q_table, walls, density)
    return remote(
        settle_kernel,
        3,
        smem(2) + vmem(1),
        (jax.ShapeDtypeStruct((6, cells, width), f32), jax.ShapeDtypeStruct((cells, width), f32)),
        [
            pltpu.VMEM((peer_count * capacity, 8, width), f32),
            pltpu.VMEM((cells + peer_count * capacity, 8, width), f32),
        ]
        + sems[:2],
    )(picks, order, moved)


def solution(mesh):
    return jax.shard_map(
        shards,
        mesh=mesh,
        in_specs=(
            P(None, ("group", "dev"), None),
            P(None, ("group", "dev"), None),
            P(("group", "dev"), None),
            P(("group", "dev")),
            P(("group", "dev"), None),
            P(("group", "dev"), None),
            P("group", "dev", None, None),
            P("group", None),
        ),
        out_specs=(P(None, ("group", "dev"), None), P(("group", "dev"), None)),
        check_vma=False,
    )
```

```python
import jax
import jax.numpy as jnp
from jax import lax
from jax.experimental import pallas as pl
from jax.experimental.pallas import tpu as pltpu
from jax.sharding import PartitionSpec as P

RIM_CELLS = 4
MESH = pl.DeviceIdType.MESH


SUPPORT = 4.0
STIFFNESS = 2.0
REST_DENSITY = 0.8
VISCOSITY = 0.5
COHESION = 0.3
ADHESION = 0.8
GRAVITY = 1.0
TIME_STEP = 0.5


def coarse(a):
    return a.astype(jnp.bfloat16).astype(jnp.float32)


def split3(a):
    high = coarse(a)
    rest = a - high
    mid = coarse(rest)
    return high, mid, coarse(rest - mid)


def source_side(pos, scale):
    square = jnp.sum(pos * pos, axis=0, keepdims=True)
    rows = jnp.concatenate(
        [
            scale * (1.0 - square / SUPPORT),
            scale / SUPPORT,
            scale * pos * (2.0 / SUPPORT),
            jnp.zeros_like(pos),
        ],
        0,
    )
    h, m, l = split3(rows)
    return jnp.concatenate([h, h, m, m, h, l], 0).T.astype(jnp.bfloat16)


def target_side(pos):
    square = jnp.sum(pos * pos, axis=0, keepdims=True)
    rows = jnp.concatenate([jnp.ones_like(square), -square, pos, jnp.zeros_like(pos)], 0)
    h, m, l = split3(rows)
    return jnp.concatenate([h, m, h, m, l, h], 0).astype(jnp.bfloat16)


def mm(a, b):
    return jnp.dot(a, b, preferred_element_type=jnp.float32)


HALF = 128
NEAR = 3
CLASSES = [(width, n) for width in (1, 2) for n in range(NEAR + width, 2 * NEAR + width + 1)]


def sort_cells(near, filled, lists, sizes, extra):
    cells = near.shape[0] // NEAR
    base = 2 * (NEAR + 1)
    for k in range(base * 2):
        sizes[k] = 0

    def one(c, _):
        own = filled[RIM_CELLS + c]
        count = 0
        for r in [RIM_CELLS + c] + [near[c * NEAR + k] for k in range(NEAR)]:
            extra[c * 4 + count] = r
            count = count + filled[r]
        cls = own * (NEAR + 1) + count - own
        size = sizes[cls]
        lists[cls * cells + size] = c
        sizes[cls] = size + 1
        return 0

    lax.fori_loop(0, cells, one, 0)


def by_class(lists, sizes, body, together):
    cells = lists.shape[0] // len(CLASSES)
    for cls, (width, n) in enumerate(CLASSES):
        size = sizes[cls]

        def step(k, _, cls=cls, width=width, n=n, size=size):
            for u in range(together):
                at = jnp.minimum(k * together + u, size - 1)
                body(lists[cls * cells + at], width * HALF, n)
            return 0

        lax.fori_loop(0, (size + together - 1) // together, step, 0)


def chunks(near, extra, c, n):
    rows = [RIM_CELLS + c] + [near[c * NEAR + k] for k in range(NEAR)]
    return [2 * r for r in rows] + [2 * extra[c * 4 + k] + 1 for k in range(n - NEAR - 1)]


def widen(row, width):
    if row.shape[1] == width:
        return row
    return jnp.concatenate([row, jnp.zeros((row.shape[0], width - row.shape[1]), row.dtype)], 1)


def to_peers(act):
    me, count = lax.axis_index("dev"), lax.axis_size("dev")

    def one(k, _):
        act(lax.rem(me + k, count))
        return 0

    lax.fori_loop(1, count, one, 0)


def greet(rim):
    barrier = pltpu.get_barrier_semaphore()
    group, groups = lax.axis_index("group"), lax.axis_size("group")

    def hello(p):
        pl.semaphore_signal(barrier, inc=1, device_id={"dev": p}, device_id_type=MESH)

    to_peers(hello)
    if not rim:
        return

    @pl.when(group > 0)
    def _():
        pl.semaphore_signal(barrier, inc=1, device_id={"group": group - 1}, device_id_type=MESH)

    @pl.when(group < groups - 1)
    def _():
        pl.semaphore_signal(barrier, inc=1, device_id={"group": group + 1}, device_id_type=MESH)


def greeted(rim):
    group, groups = lax.axis_index("group"), lax.axis_size("group")
    amount = lax.axis_size("dev") - 1
    if rim:
        amount = amount + jnp.where(group > 0, 1, 0) + jnp.where(group < groups - 1, 1, 0)
    pl.semaphore_wait(pltpu.get_barrier_semaphore(), amount)


def swap_slots(source, target, base, width, send_sem, recv_sem):
    me = lax.axis_index("dev")

    def copy(p, lands):
        return pltpu.make_async_remote_copy(
            src_ref=source.at[pl.ds(p * width, width)],
            dst_ref=target.at[pl.ds(base + lands * width, width)],
            send_sem=send_sem.at[p],
            recv_sem=recv_sem.at[lands],
            device_id={"dev": p},
            device_id_type=MESH,
        )

    def finish():
        to_peers(lambda p: copy(p, p).wait_recv())
        to_peers(lambda p: copy(p, me).wait_send())

    to_peers(lambda p: copy(p, me).start())
    return finish


def swap_rims(table, cells, sems):
    group, groups = lax.axis_index("group"), lax.axis_size("group")

    def copy(up):
        source = cells if up else RIM_CELLS
        lands = 0 if up else RIM_CELLS + cells
        step = 1 if up else -1
        return pltpu.make_async_remote_copy(
            src_ref=table.at[pl.ds(source, RIM_CELLS)],
            dst_ref=table.at[pl.ds(lands, RIM_CELLS)],
            send_sem=sems.at[0 if up else 1],
            recv_sem=sems.at[2 if up else 3],
            device_id={"group": group + step},
            device_id_type=MESH,
        )

    @pl.when(group < groups - 1)
    def _():
        copy(True).start()

    @pl.when(group > 0)
    def _():
        copy(False).start()

    def finish():
        @pl.when(group < groups - 1)
        def _():
            copy(False).wait_recv()
            copy(True).wait_send()

        @pl.when(group > 0)
        def _():
            copy(True).wait_recv()
            copy(False).wait_send()

    return finish


def clear_missing(table, cells):
    group, groups = lax.axis_index("group"), lax.axis_size("group")
    shape = (RIM_CELLS,) + table.shape[1:]

    @pl.when(group == 0)
    def _():
        table[0:RIM_CELLS] = jnp.zeros(shape, jnp.float32)

    @pl.when(group == groups - 1)
    def _():
        table[RIM_CELLS + cells : 2 * RIM_CELLS + cells] = jnp.zeros(shape, jnp.float32)


def clear_own(table, base, width):
    table[pl.ds(base + lax.axis_index("dev") * width, width)] = jnp.zeros(
        (width,) + table.shape[1:], jnp.float32
    )


def fields_kernel(counts, sends, pos, vel, masses, walls, table, out, slot_send, slot_recv, rim_sem):
    cells = masses.shape[0]
    slots = out.shape[0]
    base = cells + 2 * RIM_CELLS
    width = slots // lax.axis_size("dev")

    greet(True)

    def rows(c):
        mass = masses[pl.ds(c, 1)]
        slot = lax.broadcasted_iota(jnp.int32, mass.shape, 1)
        active = (slot < counts[c]).astype(jnp.float32)
        mass = mass * active
        wall = walls[pl.ds(c, 1)].astype(jnp.float32) * active
        bond = mass * (COHESION + (ADHESION - COHESION) * wall)
        place = [pos[f, pl.ds(c, 1)] for f in range(3)]
        speed = [vel[f, pl.ds(c, 1)] for f in range(3)]
        return jnp.concatenate(place + [mass] + speed + [bond], 0)

    def own(c, _):
        table[RIM_CELLS + c] = rows(c)
        return 0

    def listed(s, _):
        c = sends[s]
        out[s] = rows(jnp.maximum(c, 0)) * (c >= 0).astype(jnp.float32)
        return 0

    lax.fori_loop(0, slots, listed, 0, unroll=4)
    lax.fori_loop(0, cells, own, 0, unroll=4)
    clear_missing(table, cells)
    clear_own(table, base, width)
    greeted(True)
    done_slots = swap_slots(out, table, base, width, slot_send, slot_recv)
    done_rims = swap_rims(table, cells, rim_sem)
    done_slots()
    done_rims()


def pressure_kernel(sends, pressure, table, out, slot_send, slot_recv, rim_sem):
    cells = pressure.shape[0]
    slots = out.shape[0]
    base = cells + 2 * RIM_CELLS
    width = slots // lax.axis_size("dev")

    greet(True)

    def listed(s, _):
        c = sends[s]
        out[s] = pressure[jnp.maximum(c, 0)] * (c >= 0).astype(jnp.float32)
        return 0

    def own(c, _):
        table[RIM_CELLS + c] = pressure[c]
        return 0

    lax.fori_loop(0, slots, listed, 0, unroll=4)
    lax.fori_loop(0, cells, own, 0, unroll=4)
    clear_missing(table, cells)
    clear_own(table, base, width)
    greeted(True)
    done_slots = swap_slots(out, table, base, width, slot_send, slot_recv)
    done_rims = swap_rims(table, cells, rim_sem)
    done_slots()
    done_rims()


def settle_kernel(picks, order, moved, state, rho, out, pool, slot_send, slot_recv):
    cells = moved.shape[0]
    slots = out.shape[0]
    width = slots // lax.axis_size("dev")

    greet(False)

    def listed(s, _):
        out[s] = moved[picks[s]]
        return 0

    def own(c, _):
        pool[c] = moved[c]
        return 0

    lax.fori_loop(0, slots, listed, 0, unroll=4)
    lax.fori_loop(0, cells, own, 0, unroll=4)
    clear_own(pool, cells, width)
    greeted(False)
    swap_slots(out, pool, cells, width, slot_send, slot_recv)()

    def place(s, _):
        row = pool[order[s]]
        for f in range(6):
            state[f, pl.ds(s, 1)] = row[f : f + 1]
        rho[pl.ds(s, 1)] = row[6:7]
        return 0

    lax.fori_loop(0, cells, place, 0, unroll=4)


def density_kernel(near, counts, filled, table, rho_ref, q_ref, lists, sizes, extra, left):
    rows_total = table.shape[0]
    full = table.shape[2]
    sort_cells(near, filled, lists, sizes, extra)

    def prepare(r, _):
        row = table[r]
        mass = row[3:4]
        root = jnp.where(mass > 0.0, jnp.exp(jnp.log(jnp.maximum(mass, 1e-30)) * (1.0 / 3.0)), 0.0)
        side = source_side(row[0:3], root)
        left[2 * r] = side[:HALF]
        left[2 * r + 1] = side[HALF:]
        return 0

    lax.fori_loop(0, rows_total, prepare, 0, unroll=8)

    def cell(c, width, n):
        right = target_side(table[RIM_CELLS + c][0:3, :width])
        total = jnp.zeros((8, width), jnp.float32)
        for k in chunks(near, extra, c, n):
            u = jnp.maximum(mm(left[k], right), 0.0)
            total = total + jnp.sum((u * u * u).reshape(-1, 8, width), axis=0)
        rho = jnp.sum(total, axis=0, keepdims=True)
        slot = lax.broadcasted_iota(jnp.int32, rho.shape, 1)
        active = (slot < counts[c]).astype(jnp.float32)
        safe = active * rho + (1.0 - active)
        rho_ref[c] = widen(rho, full)
        q_ref[c] = widen(active * STIFFNESS * (rho - REST_DENSITY) / (safe * safe), full)

    by_class(lists, sizes, cell, 2)


def force_kernel(
    near, counts, lists, sizes, extra, table, q_table, walls, rho_ref, out_ref, left, red_a, red_b
):
    rows_total = table.shape[0]
    full = table.shape[2]

    def prepare(r, _):
        row = table[r]
        pos, mass, vel, bond = row[0:3], row[3:4], row[4:7], row[7:8]
        side = source_side(pos, jnp.ones_like(mass))
        mq = mass * q_table[r]
        two = jnp.concatenate([mass, mass * pos, mq, mq * pos], 0)
        one = jnp.concatenate([bond, bond * pos, mass, mass * vel], 0)
        h2 = coarse(two)
        h1 = coarse(one)
        l1 = one - h1
        r2 = jnp.concatenate([h2, two - h2], 0)
        r1 = jnp.concatenate([h1[0:4], l1[0:4]], 0)
        r3 = jnp.concatenate([h1[4:8], l1[4:8]], 0)
        none = jnp.zeros((8, HALF), jnp.float32)
        for k in range(2):
            part = slice(k * HALF, (k + 1) * HALF)
            left[2 * r + k] = side[part]
            red_a[2 * r + k] = jnp.concatenate([r2[:, part]] * 2, 1).astype(jnp.bfloat16)
            red_b[2 * r + k] = jnp.concatenate(
                [jnp.concatenate([r1[:, part], none], 1), jnp.concatenate([none, r3[:, part]], 1)], 0
            ).astype(jnp.bfloat16)
        return 0

    lax.fori_loop(0, rows_total, prepare, 0, unroll=8)

    def cell(c, width, n):
        row = table[RIM_CELLS + c][:, :width]
        pos, vel = row[0:3], row[4:7]
        right = target_side(pos)
        s2 = jnp.zeros((16, width), jnp.float32)
        s13 = jnp.zeros((16, width), jnp.float32)
        for k in chunks(near, extra, c, n):
            w = jnp.maximum(mm(left[k], right), 0.0)
            w2 = w * w
            w3 = w2 * w
            high = w2.astype(jnp.bfloat16)
            low = (w2 - high.astype(jnp.float32)).astype(jnp.bfloat16)
            pair_a = jnp.concatenate([high, low], 0)
            pair_b = jnp.concatenate([w.astype(jnp.bfloat16), w3.astype(jnp.bfloat16)], 0)
            if width == HALF:
                both = mm(
                    jnp.concatenate([red_a[k], red_b[k]], 0), jnp.concatenate([pair_a, pair_b], 1)
                )
                s2 = s2 + both[:16, :HALF]
                s13 = s13 + both[16:, HALF:]
            else:
                s2 = s2 + mm(red_a[k], pair_a)
                s13 = s13 + mm(red_b[k], pair_b)
        s1, s3 = s13[0:8], s13[8:16]
        s2 = s2[0:8] + s2[8:16]
        s1 = s1[0:4] + s1[4:8]
        s3 = s3[0:4] + s3[4:8]
        q = q_table[RIM_CELLS + c][:, :width]
        acc = (
            (6.0 / SUPPORT) * (q * (pos * s2[0:1] - s2[1:4]) + (pos * s2[4:5] - s2[5:8]))
            - (pos * s1[0:1] - s1[1:4])
            + VISCOSITY * (s3[1:4] - vel * s3[0:1])
        )
        component = lax.broadcasted_iota(jnp.int32, acc.shape, 0)
        acc = acc - jnp.where(component == 2, GRAVITY, 0.0)
        slot = lax.broadcasted_iota(jnp.int32, q.shape, 1)
        active = (slot < counts[c]).astype(jnp.float32)
        fluid = active - walls[pl.ds(c, 1)][:, :width].astype(jnp.float32) * active
        new_vel = vel + TIME_STEP * fluid * acc
        new_pos = pos + TIME_STEP * fluid * new_vel
        rho = rho_ref[c][:, :width]
        out_ref[c] = widen(
            active * jnp.concatenate([new_pos, new_vel, rho, jnp.zeros_like(rho)], 0), full
        )

    by_class(lists, sizes, cell, 1)


def vmem(count):
    return [pl.BlockSpec(memory_space=pltpu.VMEM)] * count


def smem(count):
    return [pl.BlockSpec(memory_space=pltpu.SMEM)] * count


def densities(near, counts, filled, table, cells):
    rows, _, width = table.shape
    shape = jax.ShapeDtypeStruct((cells, 1, width), jnp.float32)
    plan = [(len(CLASSES) * cells,), (4 * (NEAR + 1),), (4 * cells,)]
    return pl.pallas_call(
        density_kernel,
        out_shape=(shape, shape) + tuple(jax.ShapeDtypeStruct(p, jnp.int32) for p in plan),
        in_specs=smem(3) + vmem(1),
        out_specs=tuple(vmem(2) + smem(3)),
        scratch_shapes=[pltpu.VMEM((rows * 2, HALF, 48), jnp.bfloat16)],
        compiler_params=pltpu.CompilerParams(vmem_limit_bytes=48 * 2**20),
    )(near, counts, filled, table)


def forces(near, counts, plan, table, q_table, walls, rho):
    rows, _, width = table.shape
    return pl.pallas_call(
        force_kernel,
        out_shape=jax.ShapeDtypeStruct((rho.shape[0], 8, width), jnp.float32),
        in_specs=smem(5) + vmem(4),
        out_specs=vmem(1)[0],
        scratch_shapes=[pltpu.VMEM((rows * 2, HALF, 48), jnp.bfloat16)]
        + [pltpu.VMEM((rows * 2, 16, 2 * HALF), jnp.bfloat16)] * 2,
        compiler_params=pltpu.CompilerParams(vmem_limit_bytes=48 * 2**20),
    )(near, counts, *plan, table, q_table, walls, rho)


def remote(kernel, collective_id, in_specs, out_shape, scratch):
    single = not isinstance(out_shape, tuple)
    return pl.pallas_call(
        kernel,
        out_shape=out_shape,
        in_specs=in_specs,
        out_specs=vmem(1)[0] if single else tuple(vmem(len(out_shape))),
        scratch_shapes=scratch,
        compiler_params=pltpu.CompilerParams(
            collective_id=collective_id, has_side_effects=True, vmem_limit_bytes=32 * 2**20
        ),
    )


def shards(positions, velocities, masses, counts, walls, neighbours, send_cells, owners):
    cells = positions.shape[1]
    width = positions.shape[2]
    peer_count = lax.axis_size("dev")
    me = lax.axis_index("dev")
    f32 = jnp.float32
    sends = send_cells.reshape(-1)
    slots = sends.shape[0]
    rows = 2 * RIM_CELLS + cells + slots
    near = neighbours.reshape(-1)
    dma = pltpu.SemaphoreType.DMA
    sems = [dma((peer_count,)), dma((peer_count,)), dma((4,))]

    capacity = max(2, cells // (2 * peer_count))
    everyone = owners[0]
    mine = lax.dynamic_slice_in_dim(everyone, me * cells, cells)
    index = jnp.arange(cells, dtype=jnp.int32)
    earlier = (mine[None, :] == mine[:, None]) & (index[None, :] < index[:, None])
    key = mine * cells + jnp.sum(earlier.astype(jnp.int32), 1)
    slot = jnp.arange(peer_count * capacity, dtype=jnp.int32)
    wanted = slot // capacity * cells + slot % capacity
    picks = jnp.sum(jnp.where(key[None, :] == wanted[:, None], index[None, :], 0), 1)
    comes = everyone.reshape(peer_count, cells) == me
    rank = jnp.sum(
        (comes[:, None, :] & (index[None, None, :] < index[None, :, None])).astype(jnp.int32), 2
    )
    amounts = jnp.sum(comes.astype(jnp.int32), 1)
    device = jnp.arange(peer_count, dtype=jnp.int32)
    starts = jnp.sum(jnp.where(device[None, :] < device[:, None], amounts[None, :], 0), 1)
    code = jnp.where(
        (device == me)[:, None], index[None, :], cells + device[:, None] * capacity + rank
    )
    goal = jnp.where(comes, starts[:, None] + rank, -1)
    order = jnp.sum(
        jnp.where(goal.reshape(1, -1) == index[:, None], code.reshape(1, -1), 0), 1
    )

    table = remote(
        fields_kernel,
        1,
        smem(2) + vmem(4),
        jax.ShapeDtypeStruct((rows, 8, width), f32),
        [pltpu.VMEM((slots, 8, width), f32)] + sems,
    )(counts, sends, positions, velocities, masses, walls)
    filled = jnp.any(table[:, 3, HALF:] != 0.0, axis=1).astype(jnp.int32)
    density, pressure, *plan = densities(near, counts, filled, table, cells)
    q_table = remote(
        pressure_kernel,
        2,
        smem(1) + vmem(1),
        jax.ShapeDtypeStruct((rows, 1, width), f32),
        [pltpu.VMEM((slots, 1, width), f32)] + sems,
    )(sends, pressure)
    moved = forces(near, counts, plan, table, q_table, walls, density)
    return remote(
        settle_kernel,
        3,
        smem(2) + vmem(1),
        (jax.ShapeDtypeStruct((6, cells, width), f32), jax.ShapeDtypeStruct((cells, width), f32)),
        [
            pltpu.VMEM((peer_count * capacity, 8, width), f32),
            pltpu.VMEM((cells + peer_count * capacity, 8, width), f32),
        ]
        + sems[:2],
    )(picks, order, moved)


def solution(mesh):
    return jax.shard_map(
        shards,
        mesh=mesh,
        in_specs=(
            P(None, ("group", "dev"), None),
            P(None, ("group", "dev"), None),
            P(("group", "dev"), None),
            P(("group", "dev")),
            P(("group", "dev"), None),
            P(("group", "dev"), None),
            P("group", "dev", None, None),
            P("group", None),
        ),
        out_specs=(P(None, ("group", "dev"), None), P(("group", "dev"), None)),
        check_vma=False,
    )
```

```python
import jax
import jax.numpy as jnp
from jax import lax
from jax.experimental import pallas as pl
from jax.experimental.pallas import tpu as pltpu
from jax.sharding import PartitionSpec as P

RIM_CELLS = 4
MESH = pl.DeviceIdType.MESH


SUPPORT = 4.0
STIFFNESS = 2.0
REST_DENSITY = 0.8
VISCOSITY = 0.5
COHESION = 0.3
ADHESION = 0.8
GRAVITY = 1.0
TIME_STEP = 0.5


def coarse(a):
    return a.astype(jnp.bfloat16).astype(jnp.float32)


def split3(a):
    high = coarse(a)
    rest = a - high
    mid = coarse(rest)
    return high, mid, coarse(rest - mid)


def source_side(pos, scale):
    square = jnp.sum(pos * pos, axis=0, keepdims=True)
    rows = jnp.concatenate(
        [
            scale * (1.0 - square / SUPPORT),
            scale / SUPPORT,
            scale * pos * (2.0 / SUPPORT),
            jnp.zeros_like(pos),
        ],
        0,
    )
    h, m, l = split3(rows)
    return jnp.concatenate([h, h, m, m, h, l], 0).T.astype(jnp.bfloat16)


def target_side(pos):
    square = jnp.sum(pos * pos, axis=0, keepdims=True)
    rows = jnp.concatenate([jnp.ones_like(square), -square, pos, jnp.zeros_like(pos)], 0)
    h, m, l = split3(rows)
    return jnp.concatenate([h, m, h, m, l, h], 0).astype(jnp.bfloat16)


def mm(a, b):
    return jnp.dot(a, b, preferred_element_type=jnp.float32)


HALF = 128
NEAR = 3
CLASSES = [(width, n) for width in (1, 2) for n in range(NEAR + width, 2 * NEAR + width + 1)]


def sort_cells(near, filled, lists, sizes, extra):
    cells = near.shape[0] // NEAR
    base = 2 * (NEAR + 1)
    for k in range(base * 2):
        sizes[k] = 0

    def one(c, _):
        own = filled[RIM_CELLS + c]
        count = 0
        for r in [RIM_CELLS + c] + [near[c * NEAR + k] for k in range(NEAR)]:
            extra[c * 4 + count] = r
            count = count + filled[r]
        cls = own * (NEAR + 1) + count - own
        size = sizes[cls]
        lists[cls * cells + size] = c
        sizes[cls] = size + 1
        return 0

    lax.fori_loop(0, cells, one, 0)


def by_class(lists, sizes, body, together):
    cells = lists.shape[0] // len(CLASSES)
    for cls, (width, n) in enumerate(CLASSES):
        size = sizes[cls]

        def step(k, _, cls=cls, width=width, n=n, size=size):
            for u in range(together):
                at = jnp.minimum(k * together + u, size - 1)
                body(lists[cls * cells + at], width * HALF, n)
            return 0

        lax.fori_loop(0, (size + together - 1) // together, step, 0)


def chunks(near, extra, c, n):
    rows = [RIM_CELLS + c] + [near[c * NEAR + k] for k in range(NEAR)]
    return [2 * r for r in rows] + [2 * extra[c * 4 + k] + 1 for k in range(n - NEAR - 1)]


def widen(row, width):
    if row.shape[1] == width:
        return row
    return jnp.concatenate([row, jnp.zeros((row.shape[0], width - row.shape[1]), row.dtype)], 1)


def to_peers(act):
    me, count = lax.axis_index("dev"), lax.axis_size("dev")

    def one(k, _):
        act(lax.rem(me + k, count))
        return 0

    lax.fori_loop(1, count, one, 0)


def greet(rim):
    barrier = pltpu.get_barrier_semaphore()
    group, groups = lax.axis_index("group"), lax.axis_size("group")

    def hello(p):
        pl.semaphore_signal(barrier, inc=1, device_id={"dev": p}, device_id_type=MESH)

    to_peers(hello)
    if not rim:
        return

    @pl.when(group > 0)
    def _():
        pl.semaphore_signal(barrier, inc=1, device_id={"group": group - 1}, device_id_type=MESH)

    @pl.when(group < groups - 1)
    def _():
        pl.semaphore_signal(barrier, inc=1, device_id={"group": group + 1}, device_id_type=MESH)


def greeted(rim):
    group, groups = lax.axis_index("group"), lax.axis_size("group")
    amount = lax.axis_size("dev") - 1
    if rim:
        amount = amount + jnp.where(group > 0, 1, 0) + jnp.where(group < groups - 1, 1, 0)
    pl.semaphore_wait(pltpu.get_barrier_semaphore(), amount)


def swap_slots(source, target, base, width, send_sem, recv_sem):
    me = lax.axis_index("dev")

    def copy(p, lands):
        return pltpu.make_async_remote_copy(
            src_ref=source.at[pl.ds(p * width, width)],
            dst_ref=target.at[pl.ds(base + lands * width, width)],
            send_sem=send_sem.at[p],
            recv_sem=recv_sem.at[lands],
            device_id={"dev": p},
            device_id_type=MESH,
        )

    def finish():
        to_peers(lambda p: copy(p, p).wait_recv())
        to_peers(lambda p: copy(p, me).wait_send())

    to_peers(lambda p: copy(p, me).start())
    return finish


def swap_rims(table, cells, sems):
    group, groups = lax.axis_index("group"), lax.axis_size("group")

    def copy(up):
        source = cells if up else RIM_CELLS
        lands = 0 if up else RIM_CELLS + cells
        step = 1 if up else -1
        return pltpu.make_async_remote_copy(
            src_ref=table.at[pl.ds(source, RIM_CELLS)],
            dst_ref=table.at[pl.ds(lands, RIM_CELLS)],
            send_sem=sems.at[0 if up else 1],
            recv_sem=sems.at[2 if up else 3],
            device_id={"group": group + step},
            device_id_type=MESH,
        )

    @pl.when(group < groups - 1)
    def _():
        copy(True).start()

    @pl.when(group > 0)
    def _():
        copy(False).start()

    def finish():
        @pl.when(group < groups - 1)
        def _():
            copy(False).wait_recv()
            copy(True).wait_send()

        @pl.when(group > 0)
        def _():
            copy(True).wait_recv()
            copy(False).wait_send()

    return finish


def clear_missing(table, cells):
    group, groups = lax.axis_index("group"), lax.axis_size("group")
    shape = (RIM_CELLS,) + table.shape[1:]

    @pl.when(group == 0)
    def _():
        table[0:RIM_CELLS] = jnp.zeros(shape, jnp.float32)

    @pl.when(group == groups - 1)
    def _():
        table[RIM_CELLS + cells : 2 * RIM_CELLS + cells] = jnp.zeros(shape, jnp.float32)


def clear_own(table, base, width):
    table[pl.ds(base + lax.axis_index("dev") * width, width)] = jnp.zeros(
        (width,) + table.shape[1:], jnp.float32
    )


def fields_kernel(counts, sends, pos, vel, masses, walls, table, out, slot_send, slot_recv, rim_sem):
    cells = masses.shape[0]
    slots = out.shape[0]
    base = cells + 2 * RIM_CELLS
    width = slots // lax.axis_size("dev")

    greet(True)

    def rows(c):
        mass = masses[pl.ds(c, 1)]
        slot = lax.broadcasted_iota(jnp.int32, mass.shape, 1)
        active = (slot < counts[c]).astype(jnp.float32)
        mass = mass * active
        wall = walls[pl.ds(c, 1)].astype(jnp.float32) * active
        bond = mass * (COHESION + (ADHESION - COHESION) * wall)
        place = [pos[f, pl.ds(c, 1)] for f in range(3)]
        speed = [vel[f, pl.ds(c, 1)] for f in range(3)]
        return jnp.concatenate(place + [mass] + speed + [bond], 0)

    def own(c, _):
        table[RIM_CELLS + c] = rows(c)
        return 0

    def listed(s, _):
        c = sends[s]
        out[s] = rows(jnp.maximum(c, 0)) * (c >= 0).astype(jnp.float32)
        return 0

    lax.fori_loop(0, slots, listed, 0, unroll=4)
    lax.fori_loop(0, cells, own, 0, unroll=4)
    clear_missing(table, cells)
    clear_own(table, base, width)
    greeted(True)
    done_slots = swap_slots(out, table, base, width, slot_send, slot_recv)
    done_rims = swap_rims(table, cells, rim_sem)
    done_slots()
    done_rims()


def pressure_kernel(sends, pressure, table, out, slot_send, slot_recv, rim_sem):
    cells = pressure.shape[0]
    slots = out.shape[0]
    base = cells + 2 * RIM_CELLS
    width = slots // lax.axis_size("dev")

    greet(True)

    def listed(s, _):
        c = sends[s]
        out[s] = pressure[jnp.maximum(c, 0)] * (c >= 0).astype(jnp.float32)
        return 0

    def own(c, _):
        table[RIM_CELLS + c] = pressure[c]
        return 0

    lax.fori_loop(0, slots, listed, 0, unroll=4)
    lax.fori_loop(0, cells, own, 0, unroll=4)
    clear_missing(table, cells)
    clear_own(table, base, width)
    greeted(True)
    done_slots = swap_slots(out, table, base, width, slot_send, slot_recv)
    done_rims = swap_rims(table, cells, rim_sem)
    done_slots()
    done_rims()


def settle_kernel(picks, order, moved, state, rho, out, pool, slot_send, slot_recv):
    cells = moved.shape[0]
    slots = out.shape[0]
    width = slots // lax.axis_size("dev")

    greet(False)

    def listed(s, _):
        out[s] = moved[picks[s]]
        return 0

    def own(c, _):
        pool[c] = moved[c]
        return 0

    lax.fori_loop(0, slots, listed, 0, unroll=4)
    lax.fori_loop(0, cells, own, 0, unroll=4)
    clear_own(pool, cells, width)
    greeted(False)
    swap_slots(out, pool, cells, width, slot_send, slot_recv)()

    def place(s, _):
        row = pool[order[s]]
        for f in range(6):
            state[f, pl.ds(s, 1)] = row[f : f + 1]
        rho[pl.ds(s, 1)] = row[6:7]
        return 0

    lax.fori_loop(0, cells, place, 0, unroll=4)


def density_kernel(near, counts, filled, table, rho_ref, q_ref, lists, sizes, extra, left):
    rows_total = table.shape[0]
    full = table.shape[2]
    sort_cells(near, filled, lists, sizes, extra)

    def prepare(r, _):
        row = table[r]
        mass = row[3:4]
        root = jnp.where(mass > 0.0, jnp.exp(jnp.log(jnp.maximum(mass, 1e-30)) * (1.0 / 3.0)), 0.0)
        side = source_side(row[0:3], root)
        left[2 * r] = side[:HALF]
        left[2 * r + 1] = side[HALF:]
        return 0

    lax.fori_loop(0, rows_total, prepare, 0, unroll=8)

    def cell(c, width, n):
        right = target_side(table[RIM_CELLS + c][0:3, :width])
        total = jnp.zeros((8, width), jnp.float32)
        for k in chunks(near, extra, c, n):
            u = jnp.maximum(mm(left[k], right), 0.0)
            total = total + jnp.sum((u * u * u).reshape(-1, 8, width), axis=0)
        rho = jnp.sum(total, axis=0, keepdims=True)
        slot = lax.broadcasted_iota(jnp.int32, rho.shape, 1)
        active = (slot < counts[c]).astype(jnp.float32)
        safe = active * rho + (1.0 - active)
        rho_ref[c] = widen(rho, full)
        q_ref[c] = widen(active * STIFFNESS * (rho - REST_DENSITY) / (safe * safe), full)

    by_class(lists, sizes, cell, 2)


def force_kernel(
    near, counts, lists, sizes, extra, table, q_table, walls, rho_ref, out_ref, left, red_a, red_b
):
    rows_total = table.shape[0]
    full = table.shape[2]

    def prepare(r, _):
        row = table[r]
        pos, mass, vel, bond = row[0:3], row[3:4], row[4:7], row[7:8]
        side = source_side(pos, jnp.ones_like(mass))
        mq = mass * q_table[r]
        two = jnp.concatenate([mass, mass * pos, mq, mq * pos], 0)
        one = jnp.concatenate([bond, bond * pos, mass, mass * vel], 0)
        h2 = coarse(two)
        h1 = coarse(one)
        l1 = one - h1
        r2 = jnp.concatenate([h2, two - h2], 0)
        r1 = jnp.concatenate([h1[0:4], l1[0:4]], 0)
        r3 = jnp.concatenate([h1[4:8], l1[4:8]], 0)
        none = jnp.zeros((8, HALF), jnp.float32)
        for k in range(2):
            part = slice(k * HALF, (k + 1) * HALF)
            left[2 * r + k] = side[part]
            red_a[2 * r + k] = jnp.concatenate([r2[:, part]] * 2, 1).astype(jnp.bfloat16)
            red_b[2 * r + k] = jnp.concatenate(
                [jnp.concatenate([r1[:, part], none], 1), jnp.concatenate([none, r3[:, part]], 1)], 0
            ).astype(jnp.bfloat16)
        return 0

    lax.fori_loop(0, rows_total, prepare, 0, unroll=8)

    def cell(c, width, n):
        row = table[RIM_CELLS + c][:, :width]
        pos, vel = row[0:3], row[4:7]
        right = target_side(pos)
        s2 = jnp.zeros((16, width), jnp.float32)
        s13 = jnp.zeros((16, width), jnp.float32)
        for k in chunks(near, extra, c, n):
            w = jnp.maximum(mm(left[k], right), 0.0)
            w2 = w * w
            w3 = w2 * w
            high = w2.astype(jnp.bfloat16)
            low = (w2 - high.astype(jnp.float32)).astype(jnp.bfloat16)
            pair_a = jnp.concatenate([high, low], 0)
            pair_b = jnp.concatenate([w.astype(jnp.bfloat16), w3.astype(jnp.bfloat16)], 0)
            if width == HALF:
                both = mm(
                    jnp.concatenate([red_a[k], red_b[k]], 0), jnp.concatenate([pair_a, pair_b], 1)
                )
                s2 = s2 + both[:16, :HALF]
                s13 = s13 + both[16:, HALF:]
            else:
                s2 = s2 + mm(red_a[k], pair_a)
                s13 = s13 + mm(red_b[k], pair_b)
        s1, s3 = s13[0:8], s13[8:16]
        s2 = s2[0:8] + s2[8:16]
        s1 = s1[0:4] + s1[4:8]
        s3 = s3[0:4] + s3[4:8]
        q = q_table[RIM_CELLS + c][:, :width]
        acc = (
            (6.0 / SUPPORT) * (q * (pos * s2[0:1] - s2[1:4]) + (pos * s2[4:5] - s2[5:8]))
            - (pos * s1[0:1] - s1[1:4])
            + VISCOSITY * (s3[1:4] - vel * s3[0:1])
        )
        component = lax.broadcasted_iota(jnp.int32, acc.shape, 0)
        acc = acc - jnp.where(component == 2, GRAVITY, 0.0)
        slot = lax.broadcasted_iota(jnp.int32, q.shape, 1)
        active = (slot < counts[c]).astype(jnp.float32)
        fluid = active - walls[pl.ds(c, 1)][:, :width].astype(jnp.float32) * active
        new_vel = vel + TIME_STEP * fluid * acc
        new_pos = pos + TIME_STEP * fluid * new_vel
        rho = rho_ref[c][:, :width]
        out_ref[c] = widen(
            active * jnp.concatenate([new_pos, new_vel, rho, jnp.zeros_like(rho)], 0), full
        )

    by_class(lists, sizes, cell, 2)


def vmem(count):
    return [pl.BlockSpec(memory_space=pltpu.VMEM)] * count


def smem(count):
    return [pl.BlockSpec(memory_space=pltpu.SMEM)] * count


def densities(near, counts, filled, table, cells):
    rows, _, width = table.shape
    shape = jax.ShapeDtypeStruct((cells, 1, width), jnp.float32)
    plan = [(len(CLASSES) * cells,), (4 * (NEAR + 1),), (4 * cells,)]
    return pl.pallas_call(
        density_kernel,
        out_shape=(shape, shape) + tuple(jax.ShapeDtypeStruct(p, jnp.int32) for p in plan),
        in_specs=smem(3) + vmem(1),
        out_specs=tuple(vmem(2) + smem(3)),
        scratch_shapes=[pltpu.VMEM((rows * 2, HALF, 48), jnp.bfloat16)],
        compiler_params=pltpu.CompilerParams(vmem_limit_bytes=48 * 2**20),
    )(near, counts, filled, table)


def forces(near, counts, plan, table, q_table, walls, rho):
    rows, _, width = table.shape
    return pl.pallas_call(
        force_kernel,
        out_shape=jax.ShapeDtypeStruct((rho.shape[0], 8, width), jnp.float32),
        in_specs=smem(5) + vmem(4),
        out_specs=vmem(1)[0],
        scratch_shapes=[pltpu.VMEM((rows * 2, HALF, 48), jnp.bfloat16)]
        + [pltpu.VMEM((rows * 2, 16, 2 * HALF), jnp.bfloat16)] * 2,
        compiler_params=pltpu.CompilerParams(vmem_limit_bytes=48 * 2**20),
    )(near, counts, *plan, table, q_table, walls, rho)


def remote(kernel, collective_id, in_specs, out_shape, scratch):
    single = not isinstance(out_shape, tuple)
    return pl.pallas_call(
        kernel,
        out_shape=out_shape,
        in_specs=in_specs,
        out_specs=vmem(1)[0] if single else tuple(vmem(len(out_shape))),
        scratch_shapes=scratch,
        compiler_params=pltpu.CompilerParams(
            collective_id=collective_id, has_side_effects=True, vmem_limit_bytes=32 * 2**20
        ),
    )


def shards(positions, velocities, masses, counts, walls, neighbours, send_cells, owners):
    cells = positions.shape[1]
    width = positions.shape[2]
    peer_count = lax.axis_size("dev")
    me = lax.axis_index("dev")
    f32 = jnp.float32
    sends = send_cells.reshape(-1)
    slots = sends.shape[0]
    rows = 2 * RIM_CELLS + cells + slots
    near = neighbours.reshape(-1)
    dma = pltpu.SemaphoreType.DMA
    sems = [dma((peer_count,)), dma((peer_count,)), dma((4,))]

    capacity = max(2, cells // (2 * peer_count))
    everyone = owners[0]
    mine = lax.dynamic_slice_in_dim(everyone, me * cells, cells)
    index = jnp.arange(cells, dtype=jnp.int32)
    earlier = (mine[None, :] == mine[:, None]) & (index[None, :] < index[:, None])
    key = mine * cells + jnp.sum(earlier.astype(jnp.int32), 1)
    slot = jnp.arange(peer_count * capacity, dtype=jnp.int32)
    wanted = slot // capacity * cells + slot % capacity
    picks = jnp.sum(jnp.where(key[None, :] == wanted[:, None], index[None, :], 0), 1)
    comes = everyone.reshape(peer_count, cells) == me
    rank = jnp.sum(
        (comes[:, None, :] & (index[None, None, :] < index[None, :, None])).astype(jnp.int32), 2
    )
    amounts = jnp.sum(comes.astype(jnp.int32), 1)
    device = jnp.arange(peer_count, dtype=jnp.int32)
    starts = jnp.sum(jnp.where(device[None, :] < device[:, None], amounts[None, :], 0), 1)
    code = jnp.where(
        (device == me)[:, None], index[None, :], cells + device[:, None] * capacity + rank
    )
    goal = jnp.where(comes, starts[:, None] + rank, -1)
    order = jnp.sum(
        jnp.where(goal.reshape(1, -1) == index[:, None], code.reshape(1, -1), 0), 1
    )

    table = remote(
        fields_kernel,
        1,
        smem(2) + vmem(4),
        jax.ShapeDtypeStruct((rows, 8, width), f32),
        [pltpu.VMEM((slots, 8, width), f32)] + sems,
    )(counts, sends, positions, velocities, masses, walls)
    filled = jnp.any(table[:, 3, HALF:] != 0.0, axis=1).astype(jnp.int32)
    density, pressure, *plan = densities(near, counts, filled, table, cells)
    q_table = remote(
        pressure_kernel,
        2,
        smem(1) + vmem(1),
        jax.ShapeDtypeStruct((rows, 1, width), f32),
        [pltpu.VMEM((slots, 1, width), f32)] + sems,
    )(sends, pressure)
    moved = forces(near, counts, plan, table, q_table, walls, density)
    return remote(
        settle_kernel,
        3,
        smem(2) + vmem(1),
        (jax.ShapeDtypeStruct((6, cells, width), f32), jax.ShapeDtypeStruct((cells, width), f32)),
        [
            pltpu.VMEM((peer_count * capacity, 8, width), f32),
            pltpu.VMEM((cells + peer_count * capacity, 8, width), f32),
        ]
        + sems[:2],
    )(picks, order, moved)


def solution(mesh):
    return jax.shard_map(
        shards,
        mesh=mesh,
        in_specs=(
            P(None, ("group", "dev"), None),
            P(None, ("group", "dev"), None),
            P(("group", "dev"), None),
            P(("group", "dev")),
            P(("group", "dev"), None),
            P(("group", "dev"), None),
            P("group", "dev", None, None),
            P("group", None),
        ),
        out_specs=(P(None, ("group", "dev"), None), P(("group", "dev"), None)),
        check_vma=False,
    )
```
